512 devices in a mesh: row: 32 (over x, y, core), col: 16 (over z).
Axes of the slice: x: 4, y: 4, z: 16, core: 2. Of those that a mesh axis runs over, the one named last changes fastest.
Arguments:
- matrix: float32 [1, 8192, 2, 4096], P(None, 'row', None, 'col'), as said below
Outputs:
- updated: float32 [1, 8192, 2, 4096], P(None, 'row', None, 'col')
Inputs may be any that keep to these rules, and one draw needn't show every extreme that they name: matrix is symmetric, and its leading 3 * 256 rows and columns form a positive definite block.
All inputs are finite; a program needn't handle non-finite values.
Results may differ from the reference program's by a relative error of at most 0.0001.
Values sent between devices are 32-bit elements; how exact they have to be, the bound alone decides.
No kernel may reach another device: no remote copies, remote signals or barrier semaphores. Data moves between devices by JAX's collectives and lax.ppermute only.
A program may use at most 64 MiB of HBM per device.

```python
import jax
import jax.numpy as jnp
from jax import lax

NB = 256
BR = 1
PANELS = 3
BC = 2
ORDER = 8192
N_ROW = 32
N_COL = 16


def draw_matrix(key, part):
    lead = PANELS * NB
    first = jax.random.fold_in(key, 0)
    second = jax.random.fold_in(key, 1)
    fourth = jax.random.fold_in(key, 3)
    noise = jax.random.normal(first, (ORDER, ORDER), jnp.float32)
    sym = (noise + noise.T) * 0.7071
    factors = jax.random.normal(fourth, (lead, lead), jnp.float32)
    dominant = jnp.exp(jax.random.uniform(second, (lead,), jnp.float32, 0.0, jnp.log(4.0)))
    gram = jnp.dot(factors, factors.T, precision=lax.Precision.HIGHEST, preferred_element_type=jnp.float32) / lead
    lead_block = gram + jnp.diag(dominant)
    lead_full = jnp.pad(lead_block, ((0, ORDER - lead), (0, ORDER - lead)))
    indices = jnp.arange(ORDER)
    inner_r = indices[:, None] < lead
    inner_c = indices[None, :] < lead
    result = jnp.where(inner_r & inner_c, lead_full, jnp.where(inner_r | inner_c, sym * 0.3, sym))
    return result.reshape(BR, N_ROW * NB, BC, N_COL * NB)


def setup_inputs(seed: int = 0) -> dict:
    key_list = jax.random.split(jax.random.key(seed), 2)
    matrix = draw_matrix(jax.random.fold_in(key_list[1], 71), 0)
    return dict(matrix=matrix)


def reference(matrix):
    full = matrix.reshape(ORDER, ORDER)
    for panel in range(PANELS):
        start = panel * NB
        stop = start + NB
        factor = jnp.linalg.cholesky(full[start:stop, start:stop])
        below = jax.scipy.linalg.solve_triangular(factor, full[stop:, start:stop].T, lower=True).T
        product = jnp.dot(below.astype(jnp.float32), below.T.astype(jnp.float32), precision=lax.Precision.HIGHEST, preferred_element_type=jnp.float32)
        full = full.at[start:stop, start:stop].set(factor)
        full = full.at[stop:, start:stop].set(below)
        full = full.at[start:stop, stop:].set(jnp.zeros((NB, ORDER - stop), jnp.float32))
        full = full.at[stop:, stop:].set(full[stop:, stop:] - product)
    return full.reshape(matrix.shape)
```

```python
import jax
import jax.numpy as jnp
from jax import lax
from jax.experimental import pallas as pl
from jax.experimental.pallas import tpu as pltpu
from jax.sharding import PartitionSpec as P

PANELS = 3
W = 128
NB = 256
N = PANELS * NB
UPPER = [(r, c) for r in range(PANELS) for c in range(r, PANELS)]


def dot(a, b, ca=1, cb=0):
    return lax.dot_general(
        a,
        b,
        (((ca,), (cb,)), ((), ())),
        precision=lax.Precision.HIGHEST,
        preferred_element_type=jnp.float32,
    )


def lane_of(x, k):
    return jnp.broadcast_to(x[:, k : k + 1], (8, W))


def row_of(x, s):
    return jnp.broadcast_to(x[s : s + 1, :], (8, W))


def factor(block):
    groups = W // 8
    lane = lax.broadcasted_iota(jnp.int32, (8, W), 1)
    sub = lax.broadcasted_iota(jnp.int32, (8, W), 0)
    x = [block[8 * p : 8 * p + 8, :] for p in range(groups)]
    v = [jnp.where(lane == sub + 8 * p, 1.0, 0.0).astype(jnp.float32) for p in range(groups)]
    upper, inverse = [], []
    for p in range(groups):
        k = 8 * p
        cols = [lane_of(x[p], k + j) for j in range(8)]
        e = [[row_of(cols[j], s) if s >= j else None for j in range(8)] for s in range(8)]
        r = [row_of(x[p], j) for j in range(8)]
        z = [row_of(v[p], j) for j in range(8)]
        low = [[None] * 8 for _ in range(8)]
        inv = [None] * 8
        for j in range(8):
            inv[j] = 1.0 / e[j][j]
            for s in range(j + 1, 8):
                low[s][j] = e[s][j] * inv[j]
            for s in range(j + 1, 8):
                for t in range(j + 1, s + 1):
                    e[s][t] = e[s][t] - low[s][j] * e[t][j]
                r[s] = r[s] - low[s][j] * r[j]
                z[s] = z[s] - low[s][j] * z[j]
        sr = [r[j] * inv[j] for j in range(8)]
        sz = [z[j] * inv[j] for j in range(8)]
        for q in range(p + 1, groups):
            c = [lane_of(x[q], k + j) for j in range(8)]
            for j in range(8):
                for s in range(j + 1, 8):
                    c[s] = c[s] - low[s][j] * c[j]
            ax, av = c[0] * sr[0], c[0] * sz[0]
            for j in range(1, 8):
                ax, av = ax + c[j] * sr[j], av + c[j] * sz[j]
            x[q], v[q] = x[q] - ax, v[q] - av
        root = lax.rsqrt(e[0][0])
        u, w = r[0] * root, z[0] * root
        for j in range(1, 8):
            root = lax.rsqrt(e[j][j])
            u, w = jnp.where(sub == j, r[j] * root, u), jnp.where(sub == j, z[j] * root, w)
        upper.append(jnp.where(lane >= sub + k, u, 0.0))
        inverse.append(w)
    return jnp.concatenate(upper, 0), jnp.concatenate(inverse, 0)


def lead_kernel(a_ref, u_ref, v_ref, s_ref):
    s_ref[...] = jnp.zeros_like(s_ref)
    for n, (r, c) in enumerate(UPPER):
        s_ref[NB * r : NB * r + NB, NB * c : NB * c + NB] = a_ref[:, n, :, :].reshape(NB, NB)
    u_ref[...] = jnp.zeros_like(u_ref)
    v_ref[...] = jnp.zeros_like(v_ref)

    def body(b, carry):
        o = pl.multiple_of(b * W, W)
        upper, inverse = factor(s_ref[pl.ds(o, W), pl.ds(o, W)])
        v_ref[pl.ds(o, W), pl.ds(pl.multiple_of((b % 2) * W, W), W)] = inverse
        rest = dot(inverse, s_ref[pl.ds(o, W), :])
        lane = lax.broadcasted_iota(jnp.int32, rest.shape, 1)
        rest = jnp.where(lane >= o + W, rest, 0.0)
        u_ref[pl.ds(o, W), :] = rest
        u_ref[pl.ds(o, W), pl.ds(o, W)] = upper
        s_ref[...] = s_ref[...] - dot(rest, rest, 0, 0)
        return carry

    lax.fori_loop(0, N // W, body, 0)
    for k in range(PANELS):
        o, m = NB * k, NB * k + W
        cross = dot(u_ref[o : o + W, m : m + W], v_ref[o : o + W, 0:W], 0, 0)
        v_ref[m : m + W, 0:W] = -dot(v_ref[m : m + W, W:NB], cross)


def update_kernel(place_ref, t_ref, p_ref, u_ref, v_ref, m_ref, o_ref, w_ref, y_ref):
    i, c = place_ref[0], place_ref[1]
    for k in range(PANELS):
        o = NB * k
        t = t_ref[:, k, :, :].reshape(NB, 2 * NB)
        y = p_ref[k]
        if k:
            t = t - dot(u_ref[0:o, o : o + NB], w_ref[0:o, :], 0, 0)
            y = y - dot(y_ref[:, 0:o], u_ref[0:o, o : o + NB])
        w_ref[o : o + NB, :] = dot(v_ref[o : o + NB, :], t)
        y_ref[:, o : o + NB] = dot(y, v_ref[o : o + NB, :], 1, 1)

    @pl.when(i < PANELS)
    def _():
        y_ref[...] = u_ref[:, pl.ds(pl.multiple_of(jnp.minimum(i, PANELS - 1) * NB, NB), NB)].T

    product = dot(y_ref[...], w_ref[...])
    keep = i >= PANELS
    o_ref[1] = jnp.where(keep, m_ref[1] - product[:, NB:], 0.0)

    @pl.when(c >= PANELS)
    def _():
        o_ref[0] = jnp.where(keep, m_ref[0] - product[:, :NB], 0.0)

    @pl.when(c < PANELS)
    def _():
        o_ref[0] = y_ref[:, pl.ds(pl.multiple_of(jnp.minimum(c, PANELS - 1) * NB, NB), NB)]


def shards(matrix):
    rows_n = lax.axis_size("row")
    my_row = lax.axis_index("row")
    my_col = lax.axis_index("col")
    step = NB // rows_n
    mine = matrix[0].transpose(1, 0, 2)
    panel = lax.all_gather(mine[0], "col")[:PANELS]
    pieces = mine.reshape(2, rows_n, step, NB).transpose(1, 0, 2, 3)
    pieces = lax.all_to_all(pieces, "row", 0, 0)[:PANELS]
    top = jnp.concatenate([pieces[:, 0], pieces[:, 1]], -1)
    tops = lax.all_gather(top, "row")
    heads = lax.all_gather(pieces[:, 0], "col")
    head = jnp.stack([heads[c, r] for r, c in UPPER])
    lead = lax.all_to_all(jnp.broadcast_to(head[None], (rows_n,) + head.shape), "row", 0, 0)
    f32 = jnp.float32
    upper, inverse = pl.pallas_call(
        lead_kernel,
        out_shape=[jax.ShapeDtypeStruct((N, N), f32), jax.ShapeDtypeStruct((N, NB), f32)],
        scratch_shapes=[pltpu.VMEM((N, N), f32)],
        compiler_params=pltpu.CompilerParams(vmem_limit_bytes=32 << 20),
        cost_estimate=pl.CostEstimate(flops=2 << 30, bytes_accessed=8 << 20, transcendentals=0),
    )(lead)
    place = jnp.stack([my_row, my_col]).astype(jnp.int32)
    vmem = pl.BlockSpec(memory_space=pltpu.VMEM)
    out = pl.pallas_call(
        update_kernel,
        out_shape=jax.ShapeDtypeStruct((2, NB, NB), f32),
        in_specs=[pl.BlockSpec(memory_space=pltpu.SMEM)] + [vmem] * 5,
        out_specs=vmem,
        scratch_shapes=[pltpu.VMEM((N, 2 * NB), f32), pltpu.VMEM((NB, N), f32)],
        compiler_params=pltpu.CompilerParams(vmem_limit_bytes=32 << 20),
        cost_estimate=pl.CostEstimate(flops=2 << 30, bytes_accessed=8 << 20, transcendentals=0),
    )(place, tops, panel, upper, inverse, mine)
    return out.transpose(1, 0, 2)[None]


def solution(mesh):
    spec = P(None, "row", None, "col")
    return jax.shard_map(shards, mesh=mesh, in_specs=(spec,), out_specs=spec, check_vma=False)
```

```python
import jax
import jax.numpy as jnp
from jax import lax
from jax.experimental import pallas as pl
from jax.experimental.pallas import tpu as pltpu
from jax.sharding import PartitionSpec as P

PANELS = 3
W = 128
NB = 256
N = PANELS * NB
UPPER = [(r, c) for c in range(PANELS) for r in range(c + 1)]


def dot(a, b, ca=1, cb=0):
    return lax.dot_general(
        a,
        b,
        (((ca,), (cb,)), ((), ())),
        precision=lax.Precision.HIGHEST,
        preferred_element_type=jnp.float32,
    )


def lane_of(x, k):
    return jnp.broadcast_to(x[:, k : k + 1], (8, W))


def row_of(x, s):
    return jnp.broadcast_to(x[s : s + 1, :], (8, W))


def factor(block):
    groups = W // 8
    lane = lax.broadcasted_iota(jnp.int32, (8, W), 1)
    sub = lax.broadcasted_iota(jnp.int32, (8, W), 0)
    x = [block[8 * p : 8 * p + 8, :] for p in range(groups)]
    v = [jnp.where(lane == sub + 8 * p, 1.0, 0.0).astype(jnp.float32) for p in range(groups)]
    upper, inverse = [], []
    d = [lane_of(x[0], t) for t in range(8)]
    for p in range(groups):
        k = 8 * p
        later = range(p + 1, groups)
        c = {q: [lane_of(x[q], k + j) for j in range(8)] for q in later}
        ahead = [lane_of(x[p + 1], k + 8 + t) for t in range(8)] if later else None
        r = [row_of(x[p], j) for j in range(8)]
        z = [row_of(v[p], j) for j in range(8)]
        inv, root = [None] * 8, None
        for j in range(8):
            pivot = row_of(d[j], j)
            inv[j] = 1.0 / pivot
            root = lax.rsqrt(pivot) if j == 0 else jnp.where(sub == j, lax.rsqrt(pivot), root)
            for s in range(j + 1, 8):
                low = row_of(d[j], s) * inv[j]
                d[s] = d[s] - d[j] * low
                r[s] = r[s] - low * r[j]
                z[s] = z[s] - low * z[j]
                for q in later:
                    c[q][s] = c[q][s] - low * c[q][j]
        if later:
            for j in range(8):
                scaled = c[p + 1][j] * inv[j]
                for t in range(8):
                    ahead[t] = ahead[t] - c[p + 1][j] * row_of(scaled, t)
        sr = [r[j] * inv[j] for j in range(8)]
        sz = [z[j] * inv[j] for j in range(8)]
        for q in later:
            ax, av = c[q][0] * sr[0], c[q][0] * sz[0]
            for j in range(1, 8):
                ax, av = ax + c[q][j] * sr[j], av + c[q][j] * sz[j]
            x[q], v[q] = x[q] - ax, v[q] - av
        u, w = r[0], z[0]
        for j in range(1, 8):
            u, w = jnp.where(sub == j, r[j], u), jnp.where(sub == j, z[j], w)
        upper.append(jnp.where(lane >= sub + k, u * root, 0.0))
        inverse.append(w * root)
        d = ahead
    return jnp.concatenate(upper, 0), jnp.concatenate(inverse, 0)


def lead_kernel(source_ref, u_ref, v_ref, a_ref, s_ref, d_ref, row_ref, last_ref, sem):
    arrival = pltpu.make_async_copy(source_ref, a_ref, sem)
    arrival.start()
    u_ref[...] = jnp.zeros_like(u_ref)
    v_ref[...] = jnp.zeros_like(v_ref)
    arrival.wait()
    for n, (r, c) in enumerate(UPPER):
        s_ref[NB * r : NB * r + NB, NB * c : NB * c + NB] = a_ref[:, n, :, :].reshape(NB, NB)
    for r in range(1, PANELS):
        s_ref[NB * r : NB * r + NB, 0 : NB * r] = jnp.zeros((NB, NB * r), jnp.float32)
    row_ref[...] = jnp.zeros_like(row_ref)
    last_ref[...] = jnp.zeros_like(last_ref)
    d_ref[...] = s_ref[0:W, 0:W]
    lane = lax.broadcasted_iota(jnp.int32, (W, N), 1)

    def body(b, carry):
        o = pl.multiple_of(b * W, W)
        before = pl.multiple_of(jnp.maximum(b - 1, 0) * W, W)
        after = pl.multiple_of(jnp.minimum(b + 1, N // W - 1) * W, W)
        rest = dot(last_ref[...], row_ref[...])
        u_ref[pl.ds(before, W), :] = jnp.where(lane >= o, rest, u_ref[pl.ds(before, W), :])
        row_ref[...] = s_ref[pl.ds(o, W), :] - dot(u_ref[:, pl.ds(o, W)], u_ref[...], 0, 0)
        ahead = u_ref[:, pl.ds(after, W)]
        corner = s_ref[pl.ds(after, W), pl.ds(after, W)] - dot(ahead, ahead, 0, 0)
        upper, inverse = factor(d_ref[...])
        u_ref[pl.ds(o, W), pl.ds(o, W)] = upper
        v_ref[pl.ds(o, W), pl.ds(pl.multiple_of((b % 2) * W, W), W)] = inverse
        last_ref[...] = inverse
        beside = dot(inverse, row_ref[:, pl.ds(after, W)])
        d_ref[...] = corner - dot(beside, beside, 0, 0)
        return carry

    lax.fori_loop(0, N // W, body, 0)
    for k in range(PANELS):
        o, m = NB * k, NB * k + W
        cross = dot(u_ref[o : o + W, m : m + W], v_ref[o : o + W, 0:W], 0, 0)
        v_ref[m : m + W, 0:W] = -dot(v_ref[m : m + W, W:NB], cross)


def update_kernel(place_ref, tops_ref, panel_ref, u_ref, v_ref, m_ref, o_ref, t_ref, p_ref, w_ref, y_ref, sems):
    i, c = place_ref[0], place_ref[1]
    arrivals = []
    for k in range(PANELS):
        arrivals.append(pltpu.make_async_copy(tops_ref.at[:, k], t_ref.at[:, k], sems.at[0, k]))
        arrivals.append(pltpu.make_async_copy(panel_ref.at[k], p_ref.at[k], sems.at[1, k]))
    for arrival in arrivals:
        arrival.start()
    for k in range(PANELS):
        o = NB * k
        arrivals[2 * k].wait()
        arrivals[2 * k + 1].wait()
        t = jnp.concatenate([t_ref[:, k, n, :, :].reshape(NB, NB) for n in range(2)], 1)
        y = p_ref[k]
        if k:
            t = t - dot(u_ref[0:o, o : o + NB], w_ref[0:o, :], 0, 0)
            y = y - dot(y_ref[:, 0:o], u_ref[0:o, o : o + NB])
        w_ref[o : o + NB, :] = dot(v_ref[o : o + NB, :], t)
        y_ref[:, o : o + NB] = dot(y, v_ref[o : o + NB, :], 1, 1)

    @pl.when(i < PANELS)
    def _():
        y_ref[...] = u_ref[:, pl.ds(pl.multiple_of(jnp.minimum(i, PANELS - 1) * NB, NB), NB)].T

    product = dot(y_ref[...], w_ref[...])
    keep = i >= PANELS
    o_ref[1] = jnp.where(keep, m_ref[1] - product[:, NB:], 0.0)

    @pl.when(c >= PANELS)
    def _():
        o_ref[0] = jnp.where(keep, m_ref[0] - product[:, :NB], 0.0)

    @pl.when(c < PANELS)
    def _():
        o_ref[0] = y_ref[:, pl.ds(pl.multiple_of(jnp.minimum(c, PANELS - 1) * NB, NB), NB)]


def copies(array, count):
    return jnp.broadcast_to(array[None], (count,) + array.shape)


def shards(matrix):
    rows_n = lax.axis_size("row")
    my_row = lax.axis_index("row")
    my_col = lax.axis_index("col")
    step = NB // rows_n
    cols_n = lax.axis_size("col")
    mine = matrix[0].transpose(1, 0, 2)
    pieces = mine.reshape(2, rows_n, step, NB).transpose(1, 0, 2, 3)
    pieces = lax.all_to_all(pieces, "row", 0, 0)[:PANELS]
    heads = lax.all_to_all(copies(pieces[:, 0], cols_n), "col", 0, 0)
    head = jnp.concatenate([heads[c, : c + 1] for c in range(PANELS)])
    lead = lax.all_to_all(copies(head, rows_n), "row", 0, 0)
    lead, pieces = lax.optimization_barrier((lead, pieces))
    tops = lax.all_to_all(copies(pieces, rows_n), "row", 0, 0)
    panel = lax.all_gather(mine[0], "col")
    f32 = jnp.float32
    hbm = pl.BlockSpec(memory_space=pltpu.HBM)
    upper, inverse = pl.pallas_call(
        lead_kernel,
        out_shape=[jax.ShapeDtypeStruct((N, N), f32), jax.ShapeDtypeStruct((N, NB), f32)],
        in_specs=[hbm],
        scratch_shapes=[
            pltpu.VMEM(lead.shape, f32),
            pltpu.VMEM((N, N), f32),
            pltpu.VMEM((W, W), f32),
            pltpu.VMEM((W, N), f32),
            pltpu.VMEM((W, W), f32),
            pltpu.SemaphoreType.DMA,
        ],
        compiler_params=pltpu.CompilerParams(vmem_limit_bytes=56 << 20),
        cost_estimate=pl.CostEstimate(flops=2 << 30, bytes_accessed=100 << 20, transcendentals=0),
    )(lead)
    place = jnp.stack([my_row, my_col]).astype(jnp.int32)
    vmem = pl.BlockSpec(memory_space=pltpu.VMEM)
    out = pl.pallas_call(
        update_kernel,
        out_shape=jax.ShapeDtypeStruct((2, NB, NB), f32),
        in_specs=[pl.BlockSpec(memory_space=pltpu.SMEM), hbm, hbm, vmem, vmem, vmem],
        out_specs=vmem,
        scratch_shapes=[
            pltpu.VMEM(tops.shape, f32),
            pltpu.VMEM((PANELS, NB, NB), f32),
            pltpu.VMEM((N, 2 * NB), f32),
            pltpu.VMEM((NB, N), f32),
            pltpu.SemaphoreType.DMA((2, PANELS)),
        ],
        compiler_params=pltpu.CompilerParams(vmem_limit_bytes=56 << 20),
        cost_estimate=pl.CostEstimate(flops=2 << 30, bytes_accessed=8 << 20, transcendentals=0),
    )(place, tops, panel, upper, inverse, mine)
    return out.transpose(1, 0, 2)[None]


def solution(mesh):
    spec = P(None, "row", None, "col")
    return jax.shard_map(shards, mesh=mesh, in_specs=(spec,), out_specs=spec, check_vma=False)
```

```python
import jax
import jax.numpy as jnp
from jax import lax
from jax.experimental import pallas as pl
from jax.experimental.pallas import tpu as pltpu
from jax.sharding import PartitionSpec as P

PANELS = 3
W = 128
NB = 256
GROUP = 4
N = PANELS * NB
UPPER = [(r, c) for c in range(PANELS) for r in range(c + 1)]


def dot(a, b, ca=1, cb=0):
    return lax.dot_general(
        a,
        b,
        (((ca,), (cb,)), ((), ())),
        precision=lax.Precision.HIGHEST,
        preferred_element_type=jnp.float32,
    )


def lane_of(x, k):
    return jnp.broadcast_to(x[:, k : k + 1], (8, W))


def row_of(x, s):
    return jnp.broadcast_to(x[s : s + 1, :], (8, W))


def factor(block):
    groups = W // 8
    lane = lax.broadcasted_iota(jnp.int32, (8, W), 1)
    sub = lax.broadcasted_iota(jnp.int32, (8, W), 0)
    x = [block[8 * p : 8 * p + 8, :] for p in range(groups)]
    v = [jnp.where(lane == sub + 8 * p, 1.0, 0.0).astype(jnp.float32) for p in range(groups)]
    upper, inverse = [], []
    d = [lane_of(x[0], t) for t in range(8)]
    for p in range(groups):
        k = 8 * p
        later = range(p + 1, groups)
        c = {q: [lane_of(x[q], k + j) for j in range(8)] for q in later}
        ahead = [lane_of(x[p + 1], k + 8 + t) for t in range(8)] if later else None
        r = [row_of(x[p], j) for j in range(8)]
        z = [row_of(v[p], j) for j in range(8)]
        inv, root = [None] * 8, None
        for j in range(8):
            pivot = row_of(d[j], j)
            inv[j] = 1.0 / pivot
            root = lax.rsqrt(pivot) if j == 0 else jnp.where(sub == j, lax.rsqrt(pivot), root)
            for s in range(j + 1, 8):
                low = row_of(d[j], s) * inv[j]
                d[s] = d[s] - d[j] * low
                r[s] = r[s] - low * r[j]
                z[s] = z[s] - low * z[j]
                for q in later:
                    c[q][s] = c[q][s] - low * c[q][j]
        if later:
            for j in range(8):
                scaled = c[p + 1][j] * inv[j]
                for t in range(8):
                    ahead[t] = ahead[t] - c[p + 1][j] * row_of(scaled, t)
        sr = [r[j] * inv[j] for j in range(8)]
        sz = [z[j] * inv[j] for j in range(8)]
        for q in later:
            ax, av = c[q][0] * sr[0], c[q][0] * sz[0]
            for j in range(1, 8):
                ax, av = ax + c[q][j] * sr[j], av + c[q][j] * sz[j]
            x[q], v[q] = x[q] - ax, v[q] - av
        u, w = r[0], z[0]
        for j in range(1, 8):
            u, w = jnp.where(sub == j, r[j], u), jnp.where(sub == j, z[j], w)
        upper.append(jnp.where(lane >= sub + k, u * root, 0.0))
        inverse.append(w * root)
        d = ahead
    return jnp.concatenate(upper, 0), jnp.concatenate(inverse, 0)


def lead_kernel(source_ref, u_ref, v_ref, a_ref, s_ref, d_ref, row_ref, last_ref, sem):
    arrival = pltpu.make_async_copy(source_ref, a_ref, sem)
    arrival.start()
    u_ref[...] = jnp.zeros_like(u_ref)
    v_ref[...] = jnp.zeros_like(v_ref)
    arrival.wait()
    for n, (r, c) in enumerate(UPPER):
        s_ref[NB * r : NB * r + NB, NB * c : NB * c + NB] = a_ref[:, n, :, :].reshape(NB, NB)
    for r in range(1, PANELS):
        s_ref[NB * r : NB * r + NB, 0 : NB * r] = jnp.zeros((NB, NB * r), jnp.float32)
    row_ref[...] = jnp.zeros_like(row_ref)
    last_ref[...] = jnp.zeros_like(last_ref)
    d_ref[...] = s_ref[0:W, 0:W]
    lane = lax.broadcasted_iota(jnp.int32, (W, N), 1)

    def body(b, carry):
        o = pl.multiple_of(b * W, W)
        before = pl.multiple_of(jnp.maximum(b - 1, 0) * W, W)
        after = pl.multiple_of(jnp.minimum(b + 1, N // W - 1) * W, W)
        rest = dot(last_ref[...], row_ref[...])
        u_ref[pl.ds(before, W), :] = jnp.where(lane >= o, rest, u_ref[pl.ds(before, W), :])
        row_ref[...] = s_ref[pl.ds(o, W), :] - dot(u_ref[:, pl.ds(o, W)], u_ref[...], 0, 0)
        ahead = u_ref[:, pl.ds(after, W)]
        corner = s_ref[pl.ds(after, W), pl.ds(after, W)] - dot(ahead, ahead, 0, 0)
        upper, inverse = factor(d_ref[...])
        u_ref[pl.ds(o, W), pl.ds(o, W)] = upper
        v_ref[pl.ds(o, W), pl.ds(pl.multiple_of((b % 2) * W, W), W)] = inverse
        last_ref[...] = inverse
        beside = dot(inverse, row_ref[:, pl.ds(after, W)])
        d_ref[...] = corner - dot(beside, beside, 0, 0)
        return carry

    lax.fori_loop(0, N // W, body, 0)
    for k in range(PANELS):
        o, m = NB * k, NB * k + W
        cross = dot(u_ref[o : o + W, m : m + W], v_ref[o : o + W, 0:W], 0, 0)
        v_ref[m : m + W, 0:W] = -dot(v_ref[m : m + W, W:NB], cross)


def update_kernel(place_ref, tops_ref, held_ref, one_ref, two_ref, three_ref, u_ref, v_ref, m_ref, o_ref, t_ref, p_ref, w_ref, y_ref, sems):
    i, c = place_ref[0], place_ref[1]
    at = lax.rem(c, GROUP)
    arrivals = [pltpu.make_async_copy(tops_ref.at[:, k], t_ref.at[:, k], sems.at[0, k]) for k in range(PANELS)]

    def panel_copy(k, act):
        for n, ref in enumerate([held_ref, one_ref, two_ref, three_ref]):

            @pl.when(lax.rem(at + GROUP - k, GROUP) == n)
            def _():
                act(pltpu.make_async_copy(ref, p_ref.at[k], sems.at[1, k]))

    for k in range(PANELS):
        arrivals[k].start()
        panel_copy(k, lambda copy: copy.start())
    for k in range(PANELS):
        o = NB * k
        arrivals[k].wait()
        panel_copy(k, lambda copy: copy.wait())
        t = jnp.concatenate([t_ref[:, k, n, :, :].reshape(NB, NB) for n in range(2)], 1)
        y = p_ref[k]
        if k:
            t = t - dot(u_ref[0:o, o : o + NB], w_ref[0:o, :], 0, 0)
            y = y - dot(y_ref[:, 0:o], u_ref[0:o, o : o + NB])
        w_ref[o : o + NB, :] = dot(v_ref[o : o + NB, :], t)
        y_ref[:, o : o + NB] = dot(y, v_ref[o : o + NB, :], 1, 1)

    @pl.when(i < PANELS)
    def _():
        y_ref[...] = u_ref[:, pl.ds(pl.multiple_of(jnp.minimum(i, PANELS - 1) * NB, NB), NB)].T

    product = dot(y_ref[...], w_ref[...])
    keep = i >= PANELS
    o_ref[1] = jnp.where(keep, m_ref[1] - product[:, NB:], 0.0)

    @pl.when(c >= PANELS)
    def _():
        o_ref[0] = jnp.where(keep, m_ref[0] - product[:, :NB], 0.0)

    @pl.when(c < PANELS)
    def _():
        o_ref[0] = y_ref[:, pl.ds(pl.multiple_of(jnp.minimum(c, PANELS - 1) * NB, NB), NB)]


def copies(array, count):
    return jnp.broadcast_to(array[None], (count,) + array.shape)


def send(array, axis, pairs):
    return lax.ppermute(array, axis, pairs)


def shards(matrix):
    rows_n = lax.axis_size("row")
    my_row = lax.axis_index("row")
    my_col = lax.axis_index("col")
    step = NB // rows_n
    cols_n = lax.axis_size("col")
    mine = matrix[0].transpose(1, 0, 2)
    group = range(0, cols_n, GROUP)
    near = send(mine[0], "col", [(g, g + GROUP) for g in range(PANELS)])
    far = send(mine[0], "col", [(g, g + cols_n - GROUP) for g in range(PANELS)])
    pieces = mine.reshape(2, rows_n, step, NB).transpose(1, 0, 2, 3)
    pieces = lax.all_to_all(pieces, "row", 0, 0)[:PANELS]
    heads = lax.all_to_all(copies(pieces[:, 0], cols_n), "col", 0, 0)
    heads, near = lax.optimization_barrier((heads, near))
    middle = send(near, "col", [(GROUP + g, 2 * GROUP + g) for g in range(PANELS)])
    head = jnp.concatenate([heads[c, : c + 1] for c in range(PANELS)])
    lead = lax.all_to_all(copies(head, rows_n), "row", 0, 0)
    held = jnp.where(my_col < GROUP, mine[0], near + middle + far)
    lead, pieces, held = lax.optimization_barrier((lead, pieces, held))
    shifted = [
        send(held, "col", [(a + g, a + (g + n) % GROUP) for a in group for g in range(PANELS)])
        for n in range(1, GROUP)
    ]
    tops = lax.all_to_all(copies(pieces, rows_n), "row", 0, 0)
    f32 = jnp.float32
    hbm = pl.BlockSpec(memory_space=pltpu.HBM)
    upper, inverse = pl.pallas_call(
        lead_kernel,
        out_shape=[jax.ShapeDtypeStruct((N, N), f32), jax.ShapeDtypeStruct((N, NB), f32)],
        in_specs=[hbm],
        scratch_shapes=[
            pltpu.VMEM(lead.shape, f32),
            pltpu.VMEM((N, N), f32),
            pltpu.VMEM((W, W), f32),
            pltpu.VMEM((W, N), f32),
            pltpu.VMEM((W, W), f32),
            pltpu.SemaphoreType.DMA,
        ],
        compiler_params=pltpu.CompilerParams(vmem_limit_bytes=56 << 20),
        cost_estimate=pl.CostEstimate(flops=2 << 30, bytes_accessed=100 << 20, transcendentals=0),
    )(lead)
    place = jnp.stack([my_row, my_col]).astype(jnp.int32)
    vmem = pl.BlockSpec(memory_space=pltpu.VMEM)
    out = pl.pallas_call(
        update_kernel,
        out_shape=jax.ShapeDtypeStruct((2, NB, NB), f32),
        in_specs=[pl.BlockSpec(memory_space=pltpu.SMEM), hbm, hbm, hbm, hbm, hbm, vmem, vmem, vmem],
        out_specs=vmem,
        scratch_shapes=[
            pltpu.VMEM(tops.shape, f32),
            pltpu.VMEM((PANELS, NB, NB), f32),
            pltpu.VMEM((N, 2 * NB), f32),
            pltpu.VMEM((NB, N), f32),
            pltpu.SemaphoreType.DMA((2, PANELS)),
        ],
        compiler_params=pltpu.CompilerParams(vmem_limit_bytes=56 << 20),
        cost_estimate=pl.CostEstimate(flops=2 << 30, bytes_accessed=8 << 20, transcendentals=0),
    )(place, tops, held, *shifted, upper, inverse, mine)
    return out.transpose(1, 0, 2)[None]


def solution(mesh):
    spec = P(None, "row", None, "col")
    return jax.shard_map(shards, mesh=mesh, in_specs=(spec,), out_specs=spec, check_vma=False)
```

```python
import jax
import jax.numpy as jnp
from jax import lax
from jax.experimental import pallas as pl
from jax.experimental.pallas import tpu as pltpu
from jax.sharding import PartitionSpec as P

PANELS = 3
W = 128
NB = 256
N = PANELS * NB
UPPER = [(r, c) for c in range(PANELS) for r in range(c + 1)]


def dot(a, b, ca=1, cb=0):
    return lax.dot_general(
        a,
        b,
        (((ca,), (cb,)), ((), ())),
        precision=lax.Precision.HIGHEST,
        preferred_element_type=jnp.float32,
    )


def lane_of(x, k):
    return jnp.broadcast_to(x[:, k : k + 1], (8, W))


def row_of(x, s):
    return jnp.broadcast_to(x[s : s + 1, :], (8, W))


def factor(block):
    groups = W // 8
    lane = lax.broadcasted_iota(jnp.int32, (8, W), 1)
    sub = lax.broadcasted_iota(jnp.int32, (8, W), 0)
    x = [block[8 * p : 8 * p + 8, :] for p in range(groups)]
    v = [jnp.where(lane == sub + 8 * p, 1.0, 0.0).astype(jnp.float32) for p in range(groups)]
    upper, inverse = [], []
    d = [lane_of(x[0], t) for t in range(8)]
    for p in range(groups):
        k = 8 * p
        later = range(p + 1, groups)
        c = {q: [lane_of(x[q], k + j) for j in range(8)] for q in later}
        ahead = [lane_of(x[p + 1], k + 8 + t) for t in range(8)] if later else None
        r = [row_of(x[p], j) for j in range(8)]
        z = [row_of(v[p], j) for j in range(8)]
        inv, root = [None] * 8, None
        for j in range(8):
            pivot = row_of(d[j], j)
            inv[j] = 1.0 / pivot
            root = lax.rsqrt(pivot) if j == 0 else jnp.where(sub == j, lax.rsqrt(pivot), root)
            for s in range(j + 1, 8):
                low = row_of(d[j], s) * inv[j]
                d[s] = d[s] - d[j] * low
                r[s] = r[s] - low * r[j]
                z[s] = z[s] - low * z[j]
                for q in later:
                    c[q][s] = c[q][s] - low * c[q][j]
        if later:
            for j in range(8):
                scaled = c[p + 1][j] * inv[j]
                for t in range(8):
                    ahead[t] = ahead[t] - c[p + 1][j] * row_of(scaled, t)
        sr = [r[j] * inv[j] for j in range(8)]
        sz = [z[j] * inv[j] for j in range(8)]
        for q in later:
            ax, av = c[q][0] * sr[0], c[q][0] * sz[0]
            for j in range(1, 8):
                ax, av = ax + c[q][j] * sr[j], av + c[q][j] * sz[j]
            x[q], v[q] = x[q] - ax, v[q] - av
        u, w = r[0], z[0]
        for j in range(1, 8):
            u, w = jnp.where(sub == j, r[j], u), jnp.where(sub == j, z[j], w)
        upper.append(jnp.where(lane >= sub + k, u * root, 0.0))
        inverse.append(w * root)
        d = ahead
    return jnp.concatenate(upper, 0), jnp.concatenate(inverse, 0)


def lead_kernel(source_ref, u_ref, v_ref, a_ref, s_ref, d_ref, row_ref, last_ref, sem):
    arrival = pltpu.make_async_copy(source_ref, a_ref, sem)
    arrival.start()
    u_ref[...] = jnp.zeros_like(u_ref)
    v_ref[...] = jnp.zeros_like(v_ref)
    arrival.wait()
    for n, (r, c) in enumerate(UPPER):
        s_ref[NB * r : NB * r + NB, NB * c : NB * c + NB] = a_ref[:, n, :, :].reshape(NB, NB)
    for r in range(1, PANELS):
        s_ref[NB * r : NB * r + NB, 0 : NB * r] = jnp.zeros((NB, NB * r), jnp.float32)
    row_ref[...] = jnp.zeros_like(row_ref)
    last_ref[...] = jnp.zeros_like(last_ref)
    d_ref[...] = s_ref[0:W, 0:W]
    lane = lax.broadcasted_iota(jnp.int32, (W, N), 1)

    def body(b, carry):
        o = pl.multiple_of(b * W, W)
        before = pl.multiple_of(jnp.maximum(b - 1, 0) * W, W)
        after = pl.multiple_of(jnp.minimum(b + 1, N // W - 1) * W, W)
        rest = dot(last_ref[...], row_ref[...])
        u_ref[pl.ds(before, W), :] = jnp.where(lane >= o, rest, u_ref[pl.ds(before, W), :])
        row_ref[...] = s_ref[pl.ds(o, W), :] - dot(u_ref[:, pl.ds(o, W)], u_ref[...], 0, 0)
        ahead = u_ref[:, pl.ds(after, W)]
        corner = s_ref[pl.ds(after, W), pl.ds(after, W)] - dot(ahead, ahead, 0, 0)
        upper, inverse = factor(d_ref[...])
        u_ref[pl.ds(o, W), pl.ds(o, W)] = upper
        v_ref[pl.ds(o, W), pl.ds(pl.multiple_of((b % 2) * W, W), W)] = inverse
        last_ref[...] = inverse
        beside = dot(inverse, row_ref[:, pl.ds(after, W)])
        d_ref[...] = corner - dot(beside, beside, 0, 0)
        return carry

    lax.fori_loop(0, N // W, body, 0)
    for k in range(PANELS):
        o, m = NB * k, NB * k + W
        cross = dot(u_ref[o : o + W, m : m + W], v_ref[o : o + W, 0:W], 0, 0)
        v_ref[m : m + W, 0:W] = -dot(v_ref[m : m + W, W:NB], cross)


def update_kernel(place_ref, tops_ref, u_ref, v_ref, m_ref, o_ref, t_ref, w_ref, sems):
    i, c = place_ref[0], place_ref[1]
    arrivals = [pltpu.make_async_copy(tops_ref.at[:, k], t_ref.at[:, k], sems.at[k]) for k in range(PANELS)]
    for arrival in arrivals:
        arrival.start()
    for k in range(PANELS):
        o = NB * k
        arrivals[k].wait()
        t = jnp.concatenate([t_ref[:, k, n, :, :].reshape(NB, NB) for n in range(3)], 1)
        if k:
            t = t - dot(u_ref[0:o, o : o + NB], w_ref[0:o, :], 0, 0)
        w_ref[o : o + NB, :] = dot(v_ref[o : o + NB, :], t)

    @pl.when(i < PANELS)
    def _():
        w_ref[:, 2 * NB :] = u_ref[:, pl.ds(pl.multiple_of(jnp.minimum(i, PANELS - 1) * NB, NB), NB)]

    product = dot(w_ref[:, 2 * NB :], w_ref[:, : 2 * NB], 0, 0)
    keep = i >= PANELS
    o_ref[1] = jnp.where(keep, m_ref[1] - product[:, NB:], 0.0)

    @pl.when(c >= PANELS)
    def _():
        o_ref[0] = jnp.where(keep, m_ref[0] - product[:, :NB], 0.0)

    @pl.when(c < PANELS)
    def _():
        o_ref[0] = w_ref[pl.ds(pl.multiple_of(jnp.minimum(c, PANELS - 1) * NB, NB), NB), 2 * NB :].T


def copies(array, count):
    return jnp.broadcast_to(array[None], (count,) + array.shape)


def shards(matrix):
    rows_n = lax.axis_size("row")
    my_row = lax.axis_index("row")
    my_col = lax.axis_index("col")
    step = NB // rows_n
    mine = matrix[0].transpose(1, 0, 2)
    pieces = mine.reshape(2, rows_n, step, NB).transpose(1, 0, 2, 3)
    pieces = lax.all_to_all(pieces, "row", 0, 0)[:PANELS]
    wide = lax.all_gather(pieces, "col")
    head = jnp.concatenate([wide[c, : c + 1, 0] for c in range(PANELS)])
    lead = lax.all_to_all(copies(head, rows_n), "row", 0, 0)
    lead, pieces, wide = lax.optimization_barrier((lead, pieces, wide))
    theirs = wide.transpose(2, 0, 1, 3, 4).reshape(rows_n, PANELS, 1, step, NB)
    tops = jnp.concatenate([copies(pieces, rows_n), theirs], 2)
    tops = lax.all_to_all(tops, "row", 0, 0)
    f32 = jnp.float32
    hbm = pl.BlockSpec(memory_space=pltpu.HBM)
    upper, inverse = pl.pallas_call(
        lead_kernel,
        out_shape=[jax.ShapeDtypeStruct((N, N), f32), jax.ShapeDtypeStruct((N, NB), f32)],
        in_specs=[hbm],
        scratch_shapes=[
            pltpu.VMEM(lead.shape, f32),
            pltpu.VMEM((N, N), f32),
            pltpu.VMEM((W, W), f32),
            pltpu.VMEM((W, N), f32),
            pltpu.VMEM((W, W), f32),
            pltpu.SemaphoreType.DMA,
        ],
        compiler_params=pltpu.CompilerParams(vmem_limit_bytes=56 << 20),
        cost_estimate=pl.CostEstimate(flops=2 << 30, bytes_accessed=100 << 20, transcendentals=0),
    )(lead)
    place = jnp.stack([my_row, my_col]).astype(jnp.int32)
    vmem = pl.BlockSpec(memory_space=pltpu.VMEM)
    out = pl.pallas_call(
        update_kernel,
        out_shape=jax.ShapeDtypeStruct((2, NB, NB), f32),
        in_specs=[pl.BlockSpec(memory_space=pltpu.SMEM), hbm, vmem, vmem, vmem],
        out_specs=vmem,
        scratch_shapes=[pltpu.VMEM(tops.shape, f32), pltpu.VMEM((N, 3 * NB), f32), pltpu.SemaphoreType.DMA((PANELS,))],
        compiler_params=pltpu.CompilerParams(vmem_limit_bytes=56 << 20),
        cost_estimate=pl.CostEstimate(flops=2 << 30, bytes_accessed=8 << 20, transcendentals=0),
    )(place, tops, upper, inverse, mine)
    return out.transpose(1, 0, 2)[None]


def solution(mesh):
    spec = P(None, "row", None, "col")
    return jax.shard_map(shards, mesh=mesh, in_specs=(spec,), out_specs=spec, check_vma=False)
```

```python
import jax
import jax.numpy as jnp
from jax import lax
from jax.experimental import pallas as pl
from jax.experimental.pallas import tpu as pltpu
from jax.sharding import PartitionSpec as P

PANELS = 3
W = 128
NB = 256
N = PANELS * NB
UPPER = [(r, c) for c in range(PANELS) for r in range(c + 1)]


def dot(a, b, ca=1, cb=0):
    return lax.dot_general(
        a,
        b,
        (((ca,), (cb,)), ((), ())),
        precision=lax.Precision.HIGHEST,
        preferred_element_type=jnp.float32,
    )


def lane_of(x, k):
    return jnp.broadcast_to(x[:, k : k + 1], (8, W))


def row_of(x, s):
    return jnp.broadcast_to(x[s : s + 1, :], (8, W))


def factor(block):
    groups = W // 8
    lane = lax.broadcasted_iota(jnp.int32, (8, W), 1)
    sub = lax.broadcasted_iota(jnp.int32, (8, W), 0)
    x = [block[8 * p : 8 * p + 8, :] for p in range(groups)]
    v = [jnp.where(lane == sub + 8 * p, 1.0, 0.0).astype(jnp.float32) for p in range(groups)]
    upper, inverse = [], []
    d = [lane_of(x[0], t) for t in range(8)]
    for p in range(groups):
        k = 8 * p
        later = range(p + 1, groups)
        c = {q: [lane_of(x[q], k + j) for j in range(8)] for q in later}
        ahead = [lane_of(x[p + 1], k + 8 + t) for t in range(8)] if later else None
        r = [row_of(x[p], j) for j in range(8)]
        z = [row_of(v[p], j) for j in range(8)]
        inv, root = [None] * 8, None
        for j in range(8):
            pivot = row_of(d[j], j)
            inv[j] = 1.0 / pivot
            root = lax.rsqrt(pivot) if j == 0 else jnp.where(sub == j, lax.rsqrt(pivot), root)
            for s in range(j + 1, 8):
                low = row_of(d[j], s) * inv[j]
                d[s] = d[s] - d[j] * low
                r[s] = r[s] - low * r[j]
                z[s] = z[s] - low * z[j]
                for q in later:
                    c[q][s] = c[q][s] - low * c[q][j]
        if later:
            for j in range(8):
                scaled = c[p + 1][j] * inv[j]
                for t in range(8):
                    ahead[t] = ahead[t] - c[p + 1][j] * row_of(scaled, t)
        sr = [r[j] * inv[j] for j in range(8)]
        sz = [z[j] * inv[j] for j in range(8)]
        for q in later:
            ax, av = c[q][0] * sr[0], c[q][0] * sz[0]
            for j in range(1, 8):
                ax, av = ax + c[q][j] * sr[j], av + c[q][j] * sz[j]
            x[q], v[q] = x[q] - ax, v[q] - av
        u, w = r[0], z[0]
        for j in range(1, 8):
            u, w = jnp.where(sub == j, r[j], u), jnp.where(sub == j, z[j], w)
        upper.append(jnp.where(lane >= sub + k, u * root, 0.0))
        inverse.append(w * root)
        d = ahead
    return jnp.concatenate(upper, 0), jnp.concatenate(inverse, 0)


def lead_kernel(source_ref, u_ref, v_ref, a_ref, s_ref, d_ref, row_ref, last_ref, sem):
    arrival = pltpu.make_async_copy(source_ref, a_ref, sem)
    arrival.start()
    u_ref[...] = jnp.zeros_like(u_ref)
    v_ref[...] = jnp.zeros_like(v_ref)
    row_ref[...] = jnp.zeros_like(row_ref)
    last_ref[...] = jnp.zeros_like(last_ref)
    arrival.wait()
    for n, (r, c) in enumerate(UPPER):
        s_ref[NB * r : NB * r + NB, NB * c : NB * c + NB] = a_ref[:, n, :, :].reshape(NB, NB)
    for r in range(1, PANELS):
        s_ref[NB * r : NB * r + NB, 0 : NB * r] = jnp.zeros((NB, NB * r), jnp.float32)
    d_ref[...] = s_ref[0:W, 0:W]
    lane = lax.broadcasted_iota(jnp.int32, (W, N), 1)

    def body(b, carry):
        o = pl.multiple_of(b * W, W)
        before = pl.multiple_of(jnp.maximum(b - 1, 0) * W, W)
        after = pl.multiple_of(jnp.minimum(b + 1, N // W - 1) * W, W)
        second = lax.rem(b, 2) == 1
        rest = dot(last_ref[...], row_ref[...])
        u_ref[pl.ds(before, W), :] = jnp.where(lane >= o, rest, u_ref[pl.ds(before, W), :])
        above = jnp.where(second, u_ref[pl.ds(before, W), pl.ds(o, W)], 0.0)
        row_ref[...] = s_ref[pl.ds(o, W), :] - dot(above, u_ref[pl.ds(before, W), :], 0, 0)
        upper, inverse = factor(d_ref[...])
        u_ref[pl.ds(o, W), pl.ds(o, W)] = upper
        v_ref[pl.ds(o, W), pl.ds(pl.multiple_of((b % 2) * W, W), W)] = inverse
        last_ref[...] = inverse

        @pl.when(jnp.logical_not(second))
        def _():
            beside = dot(inverse, row_ref[:, pl.ds(after, W)])
            d_ref[...] = s_ref[pl.ds(after, W), pl.ds(after, W)] - dot(beside, beside, 0, 0)

        for k in range(PANELS - 1):

            @pl.when(b == 2 * k + 1)
            def _():
                e = NB * (k + 1)
                u_ref[e - W : e, e:] = dot(inverse, row_ref[:, e:])
                for f in range(e, N, NB):
                    above = u_ref[e - NB : e, f : f + NB]
                    s_ref[f : f + NB, f:] = s_ref[f : f + NB, f:] - dot(above, u_ref[e - NB : e, f:], 0, 0)
                d_ref[...] = s_ref[e : e + W, e : e + W]

        return carry

    lax.fori_loop(0, N // W, body, 0)
    for k in range(PANELS):
        o, m = NB * k, NB * k + W
        cross = dot(u_ref[o : o + W, m : m + W], v_ref[o : o + W, 0:W], 0, 0)
        v_ref[m : m + W, 0:W] = -dot(v_ref[m : m + W, W:NB], cross)


def update_kernel(place_ref, t_ref, u_ref, v_ref, m_ref, o_ref, w_ref):
    i, c = place_ref[0], place_ref[1]
    for k in range(PANELS):
        o = NB * k
        t = jnp.concatenate([t_ref[:, k, n, :, :].reshape(NB, NB) for n in range(3)], 1)
        if k:
            t = t - dot(u_ref[0:o, o : o + NB], w_ref[0:o, :], 0, 0)
        w_ref[o : o + NB, :] = dot(v_ref[o : o + NB, :], t)

    @pl.when(i < PANELS)
    def _():
        w_ref[:, 2 * NB :] = u_ref[:, pl.ds(pl.multiple_of(jnp.minimum(i, PANELS - 1) * NB, NB), NB)]

    product = dot(w_ref[:, 2 * NB :], w_ref[:, : 2 * NB], 0, 0)
    keep = i >= PANELS
    o_ref[1] = jnp.where(keep, m_ref[1] - product[:, NB:], 0.0)

    @pl.when(c >= PANELS)
    def _():
        o_ref[0] = jnp.where(keep, m_ref[0] - product[:, :NB], 0.0)

    @pl.when(c < PANELS)
    def _():
        o_ref[0] = w_ref[pl.ds(pl.multiple_of(jnp.minimum(c, PANELS - 1) * NB, NB), NB), 2 * NB :].T


def copies(array, count):
    return jnp.broadcast_to(array[None], (count,) + array.shape)


def shards(matrix):
    rows_n = lax.axis_size("row")
    my_row = lax.axis_index("row")
    my_col = lax.axis_index("col")
    step = NB // rows_n
    mine = matrix[0].transpose(1, 0, 2)
    pieces = mine.reshape(2, rows_n, step, NB).transpose(1, 0, 2, 3)
    pieces = lax.all_to_all(pieces, "row", 0, 0)[:PANELS]
    wide = lax.all_gather(pieces, "col")
    head = jnp.concatenate([wide[c, : c + 1, 0] for c in range(PANELS)])
    lead = lax.all_to_all(copies(head, rows_n), "row", 0, 0)
    theirs = wide.transpose(2, 0, 1, 3, 4).reshape(rows_n, PANELS, 1, step, NB)
    tops = jnp.concatenate([copies(pieces, rows_n), theirs], 2)
    place = jnp.stack([my_row, my_col]).astype(jnp.int32)
    lead, tops, place = lax.optimization_barrier((lead, tops, place))
    tops = lax.all_to_all(tops, "row", 0, 0)
    f32 = jnp.float32
    hbm = pl.BlockSpec(memory_space=pltpu.HBM)
    upper, inverse = pl.pallas_call(
        lead_kernel,
        out_shape=[jax.ShapeDtypeStruct((N, N), f32), jax.ShapeDtypeStruct((N, NB), f32)],
        in_specs=[hbm],
        scratch_shapes=[
            pltpu.VMEM(lead.shape, f32),
            pltpu.VMEM((N, N), f32),
            pltpu.VMEM((W, W), f32),
            pltpu.VMEM((W, N), f32),
            pltpu.VMEM((W, W), f32),
            pltpu.SemaphoreType.DMA,
        ],
        compiler_params=pltpu.CompilerParams(vmem_limit_bytes=55 << 20),
        cost_estimate=pl.CostEstimate(flops=2 << 30, bytes_accessed=100 << 20, transcendentals=0),
    )(lead)
    vmem = pl.BlockSpec(memory_space=pltpu.VMEM)
    out = pl.pallas_call(
        update_kernel,
        out_shape=jax.ShapeDtypeStruct((2, NB, NB), f32),
        in_specs=[pl.BlockSpec(memory_space=pltpu.SMEM), vmem, vmem, vmem, vmem],
        out_specs=vmem,
        scratch_shapes=[pltpu.VMEM((N, 3 * NB), f32)],
        compiler_params=pltpu.CompilerParams(vmem_limit_bytes=24 << 20),
        cost_estimate=pl.CostEstimate(flops=2 << 30, bytes_accessed=8 << 20, transcendentals=0),
    )(place, tops, upper, inverse, mine)
    return out.transpose(1, 0, 2)[None]


def solution(mesh):
    spec = P(None, "row", None, "col")
    return jax.shard_map(shards, mesh=mesh, in_specs=(spec,), out_specs=spec, check_vma=False)
```

```python
import jax
import jax.numpy as jnp
from jax import lax
from jax.experimental import pallas as pl
from jax.experimental.pallas import tpu as pltpu
from jax.sharding import PartitionSpec as P

PANELS = 3
W = 128
NB = 256
N = PANELS * NB
UPPER = [(r, c) for c in range(PANELS) for r in range(c + 1)]


def dot(a, b, ca=1, cb=0):
    return lax.dot_general(
        a,
        b,
        (((ca,), (cb,)), ((), ())),
        precision=lax.Precision.HIGHEST,
        preferred_element_type=jnp.float32,
    )


def lane_of(x, k):
    return jnp.broadcast_to(x[:, k : k + 1], (8, W))


def row_of(x, s):
    return jnp.broadcast_to(x[s : s + 1, :], (8, W))


def factor(block):
    groups = W // 8
    lane = lax.broadcasted_iota(jnp.int32, (8, W), 1)
    sub = lax.broadcasted_iota(jnp.int32, (8, W), 0)
    x = [block[8 * p : 8 * p + 8, :] for p in range(groups)]
    v = [jnp.where(lane == sub + 8 * p, 1.0, 0.0).astype(jnp.float32) for p in range(groups)]
    upper, inverse = [], []
    d = [lane_of(x[0], t) for t in range(8)]
    for p in range(groups):
        k = 8 * p
        later = range(p + 1, groups)
        c = {q: [lane_of(x[q], k + j) for j in range(8)] for q in later}
        ahead = [lane_of(x[p + 1], k + 8 + t) for t in range(8)] if later else None
        r = [row_of(x[p], j) for j in range(8)]
        z = [row_of(v[p], j) for j in range(8)]
        inv, root = [None] * 8, None
        for j in range(8):
            pivot = row_of(d[j], j)
            inv[j] = 1.0 / pivot
            root = lax.rsqrt(pivot) if j == 0 else jnp.where(sub == j, lax.rsqrt(pivot), root)
            for s in range(j + 1, 8):
                low = row_of(d[j], s) * inv[j]
                d[s] = d[s] - d[j] * low
                r[s] = r[s] - low * r[j]
                z[s] = z[s] - low * z[j]
                for q in later:
                    c[q][s] = c[q][s] - low * c[q][j]
        if later:
            for j in range(8):
                scaled = c[p + 1][j] * inv[j]
                for t in range(8):
                    ahead[t] = ahead[t] - c[p + 1][j] * row_of(scaled, t)
        sr = [r[j] * inv[j] for j in range(8)]
        sz = [z[j] * inv[j] for j in range(8)]
        for q in later:
            ax, av = c[q][0] * sr[0], c[q][0] * sz[0]
            for j in range(1, 8):
                ax, av = ax + c[q][j] * sr[j], av + c[q][j] * sz[j]
            x[q], v[q] = x[q] - ax, v[q] - av
        u, w = r[0], z[0]
        for j in range(1, 8):
            u, w = jnp.where(sub == j, r[j], u), jnp.where(sub == j, z[j], w)
        upper.append(jnp.where(lane >= sub + k, u * root, 0.0))
        inverse.append(w * root)
        d = ahead
    return jnp.concatenate(upper, 0), jnp.concatenate(inverse, 0)


def lead_kernel(source_ref, u_ref, v_ref, a_ref, s_ref, d_ref, row_ref, last_ref, sem):
    arrival = pltpu.make_async_copy(source_ref, a_ref, sem)
    arrival.start()
    u_ref[...] = jnp.zeros_like(u_ref)
    v_ref[...] = jnp.zeros_like(v_ref)
    row_ref[...] = jnp.zeros_like(row_ref)
    last_ref[...] = jnp.zeros_like(last_ref)
    arrival.wait()
    for n, (r, c) in enumerate(UPPER):
        s_ref[NB * r : NB * r + NB, NB * c : NB * c + NB] = a_ref[:, n, :, :].reshape(NB, NB)
    for r in range(1, PANELS):
        s_ref[NB * r : NB * r + NB, 0 : NB * r] = jnp.zeros((NB, NB * r), jnp.float32)
    d_ref[...] = s_ref[0:W, 0:W]
    lane = lax.broadcasted_iota(jnp.int32, (W, N), 1)

    def body(b, carry):
        o = pl.multiple_of(b * W, W)
        before = pl.multiple_of(jnp.maximum(b - 1, 0) * W, W)
        after = pl.multiple_of(jnp.minimum(b + 1, N // W - 1) * W, W)
        second = lax.rem(b, 2) == 1
        rest = dot(last_ref[...], row_ref[...])
        u_ref[pl.ds(before, W), :] = jnp.where(lane >= o, rest, u_ref[pl.ds(before, W), :])
        above = jnp.where(second, u_ref[pl.ds(before, W), pl.ds(o, W)], 0.0)
        row_ref[...] = s_ref[pl.ds(o, W), :] - dot(above, u_ref[pl.ds(before, W), :], 0, 0)
        upper, inverse = factor(d_ref[...])
        u_ref[pl.ds(o, W), pl.ds(o, W)] = upper
        v_ref[pl.ds(o, W), pl.ds(pl.multiple_of((b % 2) * W, W), W)] = inverse
        last_ref[...] = inverse

        @pl.when(jnp.logical_not(second))
        def _():
            beside = dot(inverse, row_ref[:, pl.ds(after, W)])
            d_ref[...] = s_ref[pl.ds(after, W), pl.ds(after, W)] - dot(beside, beside, 0, 0)

        for k in range(PANELS - 1):

            @pl.when(b == 2 * k + 1)
            def _():
                e = NB * (k + 1)
                u_ref[e - W : e, e:] = dot(inverse, row_ref[:, e:])
                for f in range(e, N, NB):
                    above = u_ref[e - NB : e, f : f + NB]
                    s_ref[f : f + NB, f:] = s_ref[f : f + NB, f:] - dot(above, u_ref[e - NB : e, f:], 0, 0)
                d_ref[...] = s_ref[e : e + W, e : e + W]

        return carry

    lax.fori_loop(0, N // W, body, 0)
    for k in range(PANELS):
        o, m = NB * k, NB * k + W
        cross = dot(u_ref[o : o + W, m : m + W], v_ref[o : o + W, 0:W], 0, 0)
        v_ref[m : m + W, 0:W] = -dot(v_ref[m : m + W, W:NB], cross)


def update_kernel(place_ref, t_ref, upper_ref, inverse_ref, m_ref, o_ref, w_ref, u_ref, v_ref, sems):
    i, c = place_ref[0], place_ref[1]
    arrivals = []
    for k in range(PANELS):
        o = NB * k
        rows, columns = pl.ds(o, NB), pl.ds(o, NB)
        pair = (
            pltpu.make_async_copy(inverse_ref.at[rows], v_ref.at[rows], sems.at[0, k]),
            pltpu.make_async_copy(upper_ref.at[:, columns], u_ref.at[:, columns], sems.at[1, k]),
        )
        arrivals.append(pair)
        for arrival in pair:
            arrival.start()
    for k in range(PANELS):
        o = NB * k
        for arrival in arrivals[k]:
            arrival.wait()
        t = jnp.concatenate([t_ref[:, k, n, :, :].reshape(NB, NB) for n in range(3)], 1)
        if k:
            t = t - dot(u_ref[0:o, o : o + NB], w_ref[0:o, :], 0, 0)
        w_ref[o : o + NB, :] = dot(v_ref[o : o + NB, :], t)

    @pl.when(i < PANELS)
    def _():
        w_ref[:, 2 * NB :] = u_ref[:, pl.ds(pl.multiple_of(jnp.minimum(i, PANELS - 1) * NB, NB), NB)]

    product = dot(w_ref[:, 2 * NB :], w_ref[:, : 2 * NB], 0, 0)
    keep = i >= PANELS
    o_ref[1] = jnp.where(keep, m_ref[1] - product[:, NB:], 0.0)

    @pl.when(c >= PANELS)
    def _():
        o_ref[0] = jnp.where(keep, m_ref[0] - product[:, :NB], 0.0)

    @pl.when(c < PANELS)
    def _():
        o_ref[0] = w_ref[pl.ds(pl.multiple_of(jnp.minimum(c, PANELS - 1) * NB, NB), NB), 2 * NB :].T


def copies(array, count):
    return jnp.broadcast_to(array[None], (count,) + array.shape)


def shards(matrix):
    rows_n = lax.axis_size("row")
    my_row = lax.axis_index("row")
    my_col = lax.axis_index("col")
    step = NB // rows_n
    mine = matrix[0].transpose(1, 0, 2)
    pieces = mine.reshape(2, rows_n, step, NB).transpose(1, 0, 2, 3)
    pieces = lax.all_to_all(pieces, "row", 0, 0)[:PANELS]
    wide = lax.all_gather(pieces, "col")
    head = jnp.concatenate([wide[c, : c + 1, 0] for c in range(PANELS)])
    lead = lax.all_to_all(copies(head, rows_n), "row", 0, 0)
    theirs = wide.transpose(2, 0, 1, 3, 4).reshape(rows_n, PANELS, 1, step, NB)
    tops = jnp.concatenate([copies(pieces, rows_n), theirs], 2)
    place = jnp.stack([my_row, my_col]).astype(jnp.int32)
    lead, tops, place = lax.optimization_barrier((lead, tops, place))
    tops = lax.all_to_all(tops, "row", 0, 0)
    f32 = jnp.float32
    hbm = pl.BlockSpec(memory_space=pltpu.HBM)
    upper, inverse = pl.pallas_call(
        lead_kernel,
        out_shape=[jax.ShapeDtypeStruct((N, N), f32), jax.ShapeDtypeStruct((N, NB), f32)],
        in_specs=[hbm],
        scratch_shapes=[
            pltpu.VMEM(lead.shape, f32),
            pltpu.VMEM((N, N), f32),
            pltpu.VMEM((W, W), f32),
            pltpu.VMEM((W, N), f32),
            pltpu.VMEM((W, W), f32),
            pltpu.SemaphoreType.DMA,
        ],
        compiler_params=pltpu.CompilerParams(vmem_limit_bytes=55 << 20),
        cost_estimate=pl.CostEstimate(flops=2 << 30, bytes_accessed=100 << 20, transcendentals=0),
    )(lead)
    vmem = pl.BlockSpec(memory_space=pltpu.VMEM)
    out = pl.pallas_call(
        update_kernel,
        out_shape=jax.ShapeDtypeStruct((2, NB, NB), f32),
        in_specs=[pl.BlockSpec(memory_space=pltpu.SMEM), vmem, hbm, hbm, vmem],
        out_specs=vmem,
        scratch_shapes=[
            pltpu.VMEM((N, 3 * NB), f32),
            pltpu.VMEM((N, N), f32),
            pltpu.VMEM((N, NB), f32),
            pltpu.SemaphoreType.DMA((2, PANELS)),
        ],
        compiler_params=pltpu.CompilerParams(vmem_limit_bytes=24 << 20),
        cost_estimate=pl.CostEstimate(flops=2 << 30, bytes_accessed=8 << 20, transcendentals=0),
    )(place, tops, pltpu.with_memory_space_constraint(upper, pltpu.HBM), pltpu.with_memory_space_constraint(inverse, pltpu.HBM), mine)
    return out.transpose(1, 0, 2)[None]


def solution(mesh):
    spec = P(None, "row", None, "col")
    return jax.shard_map(shards, mesh=mesh, in_specs=(spec,), out_specs=spec, check_vma=False)
```

```python
import jax
import jax.numpy as jnp
from jax import lax
from jax.experimental import pallas as pl
from jax.experimental.pallas import tpu as pltpu
from jax.sharding import PartitionSpec as P

PANELS = 3
W = 128
NB = 256
N = PANELS * NB
UPPER = [(r, c) for c in range(PANELS) for r in range(c + 1)]


def dot(a, b, ca=1, cb=0):
    return lax.dot_general(
        a,
        b,
        (((ca,), (cb,)), ((), ())),
        precision=lax.Precision.HIGHEST,
        preferred_element_type=jnp.float32,
    )


def lane_of(x, k):
    return jnp.broadcast_to(x[:, k : k + 1], (8, W))


def row_of(x, s):
    return jnp.broadcast_to(x[s : s + 1, :], (8, W))


def factor(block):
    groups = W // 8
    lane = lax.broadcasted_iota(jnp.int32, (8, W), 1)
    sub = lax.broadcasted_iota(jnp.int32, (8, W), 0)
    x = [block[8 * p : 8 * p + 8, :] for p in range(groups)]
    v = [jnp.where(lane == sub + 8 * p, 1.0, 0.0).astype(jnp.float32) for p in range(groups)]
    upper, inverse = [], []
    d = [lane_of(x[0], t) for t in range(8)]
    for p in range(groups):
        k = 8 * p
        later = range(p + 1, groups)
        c = {q: [lane_of(x[q], k + j) for j in range(8)] for q in later}
        ahead = [lane_of(x[p + 1], k + 8 + t) for t in range(8)] if later else None
        r = [row_of(x[p], j) for j in range(8)]
        z = [row_of(v[p], j) for j in range(8)]
        inv, root = [None] * 8, None
        for j in range(8):
            pivot = row_of(d[j], j)
            inv[j] = 1.0 / pivot
            root = lax.rsqrt(pivot) if j == 0 else jnp.where(sub == j, lax.rsqrt(pivot), root)
            for s in range(j + 1, 8):
                low = row_of(d[j], s) * inv[j]
                d[s] = d[s] - d[j] * low
                r[s] = r[s] - low * r[j]
                z[s] = z[s] - low * z[j]
                for q in later:
                    c[q][s] = c[q][s] - low * c[q][j]
        if later:
            for j in range(8):
                scaled = c[p + 1][j] * inv[j]
                for t in range(8):
                    ahead[t] = ahead[t] - c[p + 1][j] * row_of(scaled, t)
        sr = [r[j] * inv[j] for j in range(8)]
        sz = [z[j] * inv[j] for j in range(8)]
        for q in later:
            ax, av = c[q][0] * sr[0], c[q][0] * sz[0]
            for j in range(1, 8):
                ax, av = ax + c[q][j] * sr[j], av + c[q][j] * sz[j]
            x[q], v[q] = x[q] - ax, v[q] - av
        u, w = r[0], z[0]
        for j in range(1, 8):
            u, w = jnp.where(sub == j, r[j], u), jnp.where(sub == j, z[j], w)
        upper.append(jnp.where(lane >= sub + k, u * root, 0.0))
        inverse.append(w * root)
        d = ahead
    return jnp.concatenate(upper, 0), jnp.concatenate(inverse, 0)


def lead_kernel(source_ref, u_ref, v_ref, a_ref, s_ref, d_ref, row_ref, last_ref, sem):
    arrival = pltpu.make_async_copy(source_ref, a_ref, sem)
    arrival.start()
    u_ref[...] = jnp.zeros_like(u_ref)
    v_ref[...] = jnp.zeros_like(v_ref)
    row_ref[...] = jnp.zeros_like(row_ref)
    last_ref[...] = jnp.zeros_like(last_ref)
    arrival.wait()
    for n, (r, c) in enumerate(UPPER):
        s_ref[NB * r : NB * r + NB, NB * c : NB * c + NB] = a_ref[:, n, :, :].reshape(NB, NB)
    for r in range(1, PANELS):
        s_ref[NB * r : NB * r + NB, 0 : NB * r] = jnp.zeros((NB, NB * r), jnp.float32)
    d_ref[...] = s_ref[0:W, 0:W]
    lane = lax.broadcasted_iota(jnp.int32, (W, N), 1)

    def body(b, carry):
        o = pl.multiple_of(b * W, W)
        before = pl.multiple_of(jnp.maximum(b - 1, 0) * W, W)
        after = pl.multiple_of(jnp.minimum(b + 1, N // W - 1) * W, W)
        second = lax.rem(b, 2) == 1
        rest = dot(last_ref[...], row_ref[...])
        u_ref[pl.ds(before, W), :] = jnp.where(lane >= o, rest, u_ref[pl.ds(before, W), :])
        above = jnp.where(second, u_ref[pl.ds(before, W), pl.ds(o, W)], 0.0)
        row_ref[...] = s_ref[pl.ds(o, W), :] - dot(above, u_ref[pl.ds(before, W), :], 0, 0)
        upper, inverse = factor(d_ref[...])
        u_ref[pl.ds(o, W), pl.ds(o, W)] = upper
        v_ref[pl.ds(o, W), pl.ds(pl.multiple_of((b % 2) * W, W), W)] = inverse
        last_ref[...] = inverse

        @pl.when(jnp.logical_not(second))
        def _():
            beside = dot(inverse, row_ref[:, pl.ds(after, W)])
            d_ref[...] = s_ref[pl.ds(after, W), pl.ds(after, W)] - dot(beside, beside, 0, 0)

        for k in range(PANELS - 1):

            @pl.when(b == 2 * k + 1)
            def _():
                e = NB * (k + 1)
                u_ref[e - W : e, e:] = dot(inverse, row_ref[:, e:])
                for f in range(e, N, NB):
                    above = u_ref[e - NB : e, f : f + NB]
                    s_ref[f : f + NB, f:] = s_ref[f : f + NB, f:] - dot(above, u_ref[e - NB : e, f:], 0, 0)
                d_ref[...] = s_ref[e : e + W, e : e + W]

        return carry

    lax.fori_loop(0, N // W, body, 0)
    for k in range(PANELS):
        o, m = NB * k, NB * k + W
        cross = dot(u_ref[o : o + W, m : m + W], v_ref[o : o + W, 0:W], 0, 0)
        v_ref[m : m + W, 0:W] = -dot(v_ref[m : m + W, W:NB], cross)


def update_kernel(place_ref, t_ref, upper_ref, inverse_ref, m_ref, o_ref, w_ref, u_ref, v_ref, sems):
    i, c = place_ref[0], place_ref[1]
    own = pl.ds(pl.multiple_of(jnp.minimum(i, PANELS - 1) * NB, NB), NB)
    factors = pltpu.make_async_copy(upper_ref.at[:, own], u_ref.at[:, 0:NB], sems.at[1, 0])
    arrivals = []
    for k in range(PANELS):
        o = NB * k
        arrivals.append([pltpu.make_async_copy(inverse_ref.at[o : o + NB], v_ref.at[o : o + NB], sems.at[0, k])])
        if k:
            arrivals[k].append(
                pltpu.make_async_copy(upper_ref.at[0:o, o : o + NB], u_ref.at[0:o, o : o + NB], sems.at[1, k])
            )
        for arrival in arrivals[k]:
            arrival.start()

    @pl.when(i < PANELS)
    def _():
        factors.start()

    for k in range(PANELS):
        o = NB * k
        for arrival in arrivals[k]:
            arrival.wait()
        t = jnp.concatenate([t_ref[:, k, n, :, :].reshape(NB, NB) for n in range(3)], 1)
        if k:
            t = t - dot(u_ref[0:o, o : o + NB], w_ref[0:o, :], 0, 0)
        w_ref[o : o + NB, :] = dot(v_ref[o : o + NB, :], t)

    @pl.when(i < PANELS)
    def _():
        factors.wait()
        w_ref[:, 2 * NB :] = u_ref[:, 0:NB]

    product = dot(w_ref[:, 2 * NB :], w_ref[:, : 2 * NB], 0, 0)
    keep = i >= PANELS
    o_ref[1] = jnp.where(keep, m_ref[1] - product[:, NB:], 0.0)

    @pl.when(c >= PANELS)
    def _():
        o_ref[0] = jnp.where(keep, m_ref[0] - product[:, :NB], 0.0)

    @pl.when(c < PANELS)
    def _():
        o_ref[0] = w_ref[pl.ds(pl.multiple_of(jnp.minimum(c, PANELS - 1) * NB, NB), NB), 2 * NB :].T


def copies(array, count):
    return jnp.broadcast_to(array[None], (count,) + array.shape)


def shards(matrix):
    rows_n = lax.axis_size("row")
    my_row = lax.axis_index("row")
    my_col = lax.axis_index("col")
    step = NB // rows_n
    mine = matrix[0].transpose(1, 0, 2)
    pieces = mine.reshape(2, rows_n, step, NB).transpose(1, 0, 2, 3)
    pieces = lax.all_to_all(pieces, "row", 0, 0)[:PANELS]
    wide = lax.all_gather(pieces, "col")
    head = jnp.concatenate([wide[c, : c + 1, 0] for c in range(PANELS)])
    lead = lax.all_to_all(copies(head, rows_n), "row", 0, 0)
    theirs = wide.transpose(2, 0, 1, 3, 4).reshape(rows_n, PANELS, 1, step, NB)
    tops = jnp.concatenate([copies(pieces, rows_n), theirs], 2)
    place = jnp.stack([my_row, my_col]).astype(jnp.int32)
    lead, tops, place = lax.optimization_barrier((lead, tops, place))
    tops = lax.all_to_all(tops, "row", 0, 0)
    f32 = jnp.float32
    hbm = pl.BlockSpec(memory_space=pltpu.HBM)
    upper, inverse = pl.pallas_call(
        lead_kernel,
        out_shape=[jax.ShapeDtypeStruct((N, N), f32), jax.ShapeDtypeStruct((N, NB), f32)],
        in_specs=[hbm],
        scratch_shapes=[
            pltpu.VMEM(lead.shape, f32),
            pltpu.VMEM((N, N), f32),
            pltpu.VMEM((W, W), f32),
            pltpu.VMEM((W, N), f32),
            pltpu.VMEM((W, W), f32),
            pltpu.SemaphoreType.DMA,
        ],
        compiler_params=pltpu.CompilerParams(vmem_limit_bytes=55 << 20),
        cost_estimate=pl.CostEstimate(flops=2 << 30, bytes_accessed=100 << 20, transcendentals=0),
    )(lead)
    vmem = pl.BlockSpec(memory_space=pltpu.VMEM)
    out = pl.pallas_call(
        update_kernel,
        out_shape=jax.ShapeDtypeStruct((2, NB, NB), f32),
        in_specs=[pl.BlockSpec(memory_space=pltpu.SMEM), vmem, hbm, hbm, vmem],
        out_specs=vmem,
        scratch_shapes=[
            pltpu.VMEM((N, 3 * NB), f32),
            pltpu.VMEM((N, N), f32),
            pltpu.VMEM((N, NB), f32),
            pltpu.SemaphoreType.DMA((2, PANELS)),
        ],
        compiler_params=pltpu.CompilerParams(vmem_limit_bytes=24 << 20),
        cost_estimate=pl.CostEstimate(flops=2 << 30, bytes_accessed=8 << 20, transcendentals=0),
    )(place, tops, pltpu.with_memory_space_constraint(upper, pltpu.HBM), pltpu.with_memory_space_constraint(inverse, pltpu.HBM), mine)
    return out.transpose(1, 0, 2)[None]


def solution(mesh):
    spec = P(None, "row", None, "col")
    return jax.shard_map(shards, mesh=mesh, in_specs=(spec,), out_specs=spec, check_vma=False)
```

```python
import jax
import jax.numpy as jnp
from jax import lax
from jax.experimental import pallas as pl
from jax.experimental.pallas import tpu as pltpu
from jax.sharding import PartitionSpec as P

PANELS = 3
W = 128
NB = 256
N = PANELS * NB
UPPER = [(r, c) for c in range(PANELS) for r in range(c + 1)]


def dot(a, b, ca=1, cb=0):
    return lax.dot_general(
        a,
        b,
        (((ca,), (cb,)), ((), ())),
        precision=lax.Precision.HIGHEST,
        preferred_element_type=jnp.float32,
    )


def lane_of(x, k):
    return jnp.broadcast_to(x[:, k : k + 1], (8, W))


def row_of(x, s):
    return jnp.broadcast_to(x[s : s + 1, :], (8, W))


def factor(block):
    groups = W // 8
    lane = lax.broadcasted_iota(jnp.int32, (8, W), 1)
    sub = lax.broadcasted_iota(jnp.int32, (8, W), 0)
    x = [block[8 * p : 8 * p + 8, :] for p in range(groups)]
    v = [jnp.where(lane == sub + 8 * p, 1.0, 0.0).astype(jnp.float32) for p in range(groups)]
    upper, inverse = [], []
    d = [lane_of(x[0], t) for t in range(8)]
    for p in range(groups):
        k = 8 * p
        later = range(p + 1, groups)
        c = {q: [lane_of(x[q], k + j) for j in range(8)] for q in later}
        ahead = [lane_of(x[p + 1], k + 8 + t) for t in range(8)] if later else None
        r = [row_of(x[p], j) for j in range(8)]
        z = [row_of(v[p], j) for j in range(8)]
        inv, root = [None] * 8, None
        for j in range(8):
            pivot = row_of(d[j], j)
            inv[j] = 1.0 / pivot
            root = lax.rsqrt(pivot) if j == 0 else jnp.where(sub == j, lax.rsqrt(pivot), root)
            for s in range(j + 1, 8):
                low = row_of(d[j], s) * inv[j]
                d[s] = d[s] - d[j] * low
                r[s] = r[s] - low * r[j]
                z[s] = z[s] - low * z[j]
                for q in later:
                    c[q][s] = c[q][s] - low * c[q][j]
        if later:
            for j in range(8):
                scaled = c[p + 1][j] * inv[j]
                for t in range(8):
                    ahead[t] = ahead[t] - c[p + 1][j] * row_of(scaled, t)
        sr = [r[j] * inv[j] for j in range(8)]
        sz = [z[j] * inv[j] for j in range(8)]
        for q in later:
            ax, av = c[q][0] * sr[0], c[q][0] * sz[0]
            for j in range(1, 8):
                ax, av = ax + c[q][j] * sr[j], av + c[q][j] * sz[j]
            x[q], v[q] = x[q] - ax, v[q] - av
        u, w = r[0], z[0]
        for j in range(1, 8):
            u, w = jnp.where(sub == j, r[j], u), jnp.where(sub == j, z[j], w)
        upper.append(jnp.where(lane >= sub + k, u * root, 0.0))
        inverse.append(w * root)
        d = ahead
    return jnp.concatenate(upper, 0), jnp.concatenate(inverse, 0)


def lead_kernel(place_ref, mine_ref, other_ref, u_ref, v_ref, a_ref, s_ref, d_ref, row_ref, last_ref, sems):
    half = lax.rem(place_ref[0], 2)
    arrivals = [
        pltpu.make_async_copy(mine_ref, a_ref.at[half], sems.at[0]),
        pltpu.make_async_copy(other_ref, a_ref.at[1 - half], sems.at[1]),
    ]
    for arrival in arrivals:
        arrival.start()
    u_ref[...] = jnp.zeros_like(u_ref)
    v_ref[...] = jnp.zeros_like(v_ref)
    row_ref[...] = jnp.zeros_like(row_ref)
    last_ref[...] = jnp.zeros_like(last_ref)
    for arrival in arrivals:
        arrival.wait()
    for n, (r, c) in enumerate(UPPER):
        for h in range(2):
            o = NB * c + W * h
            s_ref[NB * r : NB * r + NB, o : o + W] = a_ref[h, :, n, :, :].reshape(NB, W)
    for r in range(1, PANELS):
        s_ref[NB * r : NB * r + NB, 0 : NB * r] = jnp.zeros((NB, NB * r), jnp.float32)
    d_ref[...] = s_ref[0:W, 0:W]
    lane = lax.broadcasted_iota(jnp.int32, (W, N), 1)

    def body(b, carry):
        o = pl.multiple_of(b * W, W)
        before = pl.multiple_of(jnp.maximum(b - 1, 0) * W, W)
        after = pl.multiple_of(jnp.minimum(b + 1, N // W - 1) * W, W)
        second = lax.rem(b, 2) == 1
        rest = dot(last_ref[...], row_ref[...])
        u_ref[pl.ds(before, W), :] = jnp.where(lane >= o, rest, u_ref[pl.ds(before, W), :])
        above = jnp.where(second, u_ref[pl.ds(before, W), pl.ds(o, W)], 0.0)
        row_ref[...] = s_ref[pl.ds(o, W), :] - dot(above, u_ref[pl.ds(before, W), :], 0, 0)
        upper, inverse = factor(d_ref[...])
        u_ref[pl.ds(o, W), pl.ds(o, W)] = upper
        v_ref[pl.ds(o, W), pl.ds(pl.multiple_of((b % 2) * W, W), W)] = inverse
        last_ref[...] = inverse

        @pl.when(jnp.logical_not(second))
        def _():
            beside = dot(inverse, row_ref[:, pl.ds(after, W)])
            d_ref[...] = s_ref[pl.ds(after, W), pl.ds(after, W)] - dot(beside, beside, 0, 0)

        for k in range(PANELS - 1):

            @pl.when(b == 2 * k + 1)
            def _():
                e = NB * (k + 1)
                u_ref[e - W : e, e:] = dot(inverse, row_ref[:, e:])
                for f in range(e, N, NB):
                    above = u_ref[e - NB : e, f : f + NB]
                    s_ref[f : f + NB, f:] = s_ref[f : f + NB, f:] - dot(above, u_ref[e - NB : e, f:], 0, 0)
                d_ref[...] = s_ref[e : e + W, e : e + W]

        return carry

    lax.fori_loop(0, N // W, body, 0)
    for k in range(PANELS):
        o, m = NB * k, NB * k + W
        cross = dot(u_ref[o : o + W, m : m + W], v_ref[o : o + W, 0:W], 0, 0)
        v_ref[m : m + W, 0:W] = -dot(v_ref[m : m + W, W:NB], cross)


def update_kernel(place_ref, t_ref, upper_ref, inverse_ref, m_ref, o_ref, w_ref, u_ref, v_ref, sems):
    i, c = place_ref[0], place_ref[1]
    own = pl.ds(pl.multiple_of(jnp.minimum(i, PANELS - 1) * NB, NB), NB)
    factors = pltpu.make_async_copy(upper_ref.at[:, own], u_ref.at[:, 0:NB], sems.at[1, 0])
    arrivals = []
    for k in range(PANELS):
        o = NB * k
        arrivals.append([pltpu.make_async_copy(inverse_ref.at[o : o + NB], v_ref.at[o : o + NB], sems.at[0, k])])
        if k:
            arrivals[k].append(
                pltpu.make_async_copy(upper_ref.at[0:o, o : o + NB], u_ref.at[0:o, o : o + NB], sems.at[1, k])
            )
        for arrival in arrivals[k]:
            arrival.start()

    @pl.when(i < PANELS)
    def _():
        factors.start()

    for k in range(PANELS):
        o = NB * k
        for arrival in arrivals[k]:
            arrival.wait()
        t = jnp.concatenate([t_ref[:, k, n, :, :].reshape(NB, NB) for n in range(3)], 1)
        if k:
            t = t - dot(u_ref[0:o, o : o + NB], w_ref[0:o, :], 0, 0)
        w_ref[o : o + NB, :] = dot(v_ref[o : o + NB, :], t)

    @pl.when(i < PANELS)
    def _():
        factors.wait()
        w_ref[:, 2 * NB :] = u_ref[:, 0:NB]

    product = dot(w_ref[:, 2 * NB :], w_ref[:, : 2 * NB], 0, 0)
    keep = i >= PANELS
    o_ref[1] = jnp.where(keep, m_ref[1] - product[:, NB:], 0.0)

    @pl.when(c >= PANELS)
    def _():
        o_ref[0] = jnp.where(keep, m_ref[0] - product[:, :NB], 0.0)

    @pl.when(c < PANELS)
    def _():
        o_ref[0] = w_ref[pl.ds(pl.multiple_of(jnp.minimum(c, PANELS - 1) * NB, NB), NB), 2 * NB :].T


def copies(array, count):
    return jnp.broadcast_to(array[None], (count,) + array.shape)


def shards(matrix):
    rows_n = lax.axis_size("row")
    my_row = lax.axis_index("row")
    my_col = lax.axis_index("col")
    step = NB // rows_n
    mine = matrix[0].transpose(1, 0, 2)
    pieces = mine.reshape(2, rows_n, step, NB).transpose(1, 0, 2, 3)
    pieces = lax.all_to_all(pieces, "row", 0, 0)[:PANELS]
    wide = lax.all_gather(pieces, "col")
    head = jnp.concatenate([wide[c, : c + 1, 0] for c in range(PANELS)])
    halves = head.reshape(len(UPPER), step, 2, W).transpose(2, 0, 1, 3)
    lead = copies(halves, rows_n // 2).reshape(rows_n, len(UPPER), step, W)
    lead = lax.all_to_all(lead, "row", 0, 0)
    theirs = wide.transpose(2, 0, 1, 3, 4).reshape(rows_n, PANELS, 1, step, NB)
    tops = jnp.concatenate([copies(pieces, rows_n), theirs], 2)
    place = jnp.stack([my_row, my_col]).astype(jnp.int32)
    lead, tops, place = lax.optimization_barrier((lead, tops, place))
    tops = lax.all_to_all(tops, "row", 0, 0)
    other = lax.ppermute(lead, "row", [(i, i ^ 1) for i in range(rows_n)])
    f32 = jnp.float32
    hbm = pl.BlockSpec(memory_space=pltpu.HBM)
    upper, inverse = pl.pallas_call(
        lead_kernel,
        out_shape=[jax.ShapeDtypeStruct((N, N), f32), jax.ShapeDtypeStruct((N, NB), f32)],
        in_specs=[pl.BlockSpec(memory_space=pltpu.SMEM), hbm, hbm],
        scratch_shapes=[
            pltpu.VMEM((2,) + lead.shape, f32),
            pltpu.VMEM((N, N), f32),
            pltpu.VMEM((W, W), f32),
            pltpu.VMEM((W, N), f32),
            pltpu.VMEM((W, W), f32),
            pltpu.SemaphoreType.DMA((2,)),
        ],
        compiler_params=pltpu.CompilerParams(vmem_limit_bytes=55 << 20),
        cost_estimate=pl.CostEstimate(flops=2 << 30, bytes_accessed=100 << 20, transcendentals=0),
    )(place, lead, other)
    vmem = pl.BlockSpec(memory_space=pltpu.VMEM)
    out = pl.pallas_call(
        update_kernel,
        out_shape=jax.ShapeDtypeStruct((2, NB, NB), f32),
        in_specs=[pl.BlockSpec(memory_space=pltpu.SMEM), vmem, hbm, hbm, vmem],
        out_specs=vmem,
        scratch_shapes=[
            pltpu.VMEM((N, 3 * NB), f32),
            pltpu.VMEM((N, N), f32),
            pltpu.VMEM((N, NB), f32),
            pltpu.SemaphoreType.DMA((2, PANELS)),
        ],
        compiler_params=pltpu.CompilerParams(vmem_limit_bytes=24 << 20),
        cost_estimate=pl.CostEstimate(flops=2 << 30, bytes_accessed=8 << 20, transcendentals=0),
    )(place, tops, pltpu.with_memory_space_constraint(upper, pltpu.HBM), pltpu.with_memory_space_constraint(inverse, pltpu.HBM), mine)
    return out.transpose(1, 0, 2)[None]


def solution(mesh):
    spec = P(None, "row", None, "col")
    return jax.shard_map(shards, mesh=mesh, in_specs=(spec,), out_specs=spec, check_vma=False)
```

```python
import jax
import jax.numpy as jnp
from jax import lax
from jax.experimental import pallas as pl
from jax.experimental.pallas import tpu as pltpu
from jax.sharding import PartitionSpec as P

PANELS = 3
W = 128
NB = 256
N = PANELS * NB
UPPER = [(r, c) for c in range(PANELS) for r in range(c + 1)]


def dot(a, b, ca=1, cb=0):
    return lax.dot_general(
        a,
        b,
        (((ca,), (cb,)), ((), ())),
        precision=lax.Precision.HIGHEST,
        preferred_element_type=jnp.float32,
    )


def lane_of(x, k):
    return jnp.broadcast_to(x[:, k : k + 1], (8, W))


def row_of(x, s):
    return jnp.broadcast_to(x[s : s + 1, :], (8, W))


def factor(block):
    groups = W // 8
    half = groups // 2
    lane = lax.broadcasted_iota(jnp.int32, (8, W), 1)
    sub = lax.broadcasted_iota(jnp.int32, (8, W), 0)
    x = [block[8 * p : 8 * p + 8, :] for p in range(groups)]
    v = [jnp.where(lane == sub + 8 * p, 1.0, 0.0).astype(jnp.float32) for p in range(groups)]
    upper, inverse = [], []
    d = [lane_of(x[0], t) for t in range(8)]
    for p in range(groups):
        k = 8 * p
        later = range(p + 1, half if p < half else groups)
        c = {q: [lane_of(x[q], k + j) for j in range(8)] for q in later}
        ahead = [lane_of(x[p + 1], k + 8 + t) for t in range(8)] if later else None
        r = [row_of(x[p], j) for j in range(8)]
        z = [row_of(v[p], j) for j in range(8)]
        inv, root = [None] * 8, None
        for j in range(8):
            pivot = row_of(d[j], j)
            inv[j] = 1.0 / pivot
            root = lax.rsqrt(pivot) if j == 0 else jnp.where(sub == j, lax.rsqrt(pivot), root)
            for s in range(j + 1, 8):
                low = row_of(d[j], s) * inv[j]
                d[s] = d[s] - d[j] * low
                r[s] = r[s] - low * r[j]
                z[s] = z[s] - low * z[j]
                for q in later:
                    c[q][s] = c[q][s] - low * c[q][j]
        if later:
            for j in range(8):
                scaled = c[p + 1][j] * inv[j]
                for t in range(8):
                    ahead[t] = ahead[t] - c[p + 1][j] * row_of(scaled, t)
        sr = [r[j] * inv[j] for j in range(8)]
        sz = [z[j] * inv[j] for j in range(8)]
        for q in later:
            ax, av = c[q][0] * sr[0], c[q][0] * sz[0]
            for j in range(1, 8):
                ax, av = ax + c[q][j] * sr[j], av + c[q][j] * sz[j]
            x[q], v[q] = x[q] - ax, v[q] - av
        u, w = r[0], z[0]
        for j in range(1, 8):
            u, w = jnp.where(sub == j, r[j], u), jnp.where(sub == j, z[j], w)
        upper.append(jnp.where(lane >= sub + k, u * root, 0.0))
        inverse.append(w * root)
        d = ahead
        if p == half - 1:
            done = jnp.concatenate([jnp.concatenate(upper, 0), jnp.concatenate(inverse, 0)], 1)
            change = dot(done[:, 8 * half : W], done, 0, 0)
            for q in range(half, groups):
                rows = change[8 * (q - half) : 8 * (q - half) + 8]
                x[q], v[q] = x[q] - rows[:, :W], v[q] - rows[:, W:]
            d = [lane_of(x[half], 8 * half + t) for t in range(8)]
    return jnp.concatenate(upper, 0), jnp.concatenate(inverse, 0)


def lead_kernel(place_ref, mine_ref, other_ref, u_ref, v_ref, a_ref, s_ref, d_ref, row_ref, last_ref, sems):
    half = lax.rem(place_ref[0], 2)
    arrivals = [
        pltpu.make_async_copy(mine_ref, a_ref.at[half], sems.at[0]),
        pltpu.make_async_copy(other_ref, a_ref.at[1 - half], sems.at[1]),
    ]
    for arrival in arrivals:
        arrival.start()
    u_ref[...] = jnp.zeros_like(u_ref)
    v_ref[...] = jnp.zeros_like(v_ref)
    row_ref[...] = jnp.zeros_like(row_ref)
    last_ref[...] = jnp.zeros_like(last_ref)
    for arrival in arrivals:
        arrival.wait()
    for n, (r, c) in enumerate(UPPER):
        for h in range(2):
            o = NB * c + W * h
            s_ref[NB * r : NB * r + NB, o : o + W] = a_ref[h, :, n, :, :].reshape(NB, W)
    for r in range(1, PANELS):
        s_ref[NB * r : NB * r + NB, 0 : NB * r] = jnp.zeros((NB, NB * r), jnp.float32)
    d_ref[...] = s_ref[0:W, 0:W]
    lane = lax.broadcasted_iota(jnp.int32, (W, N), 1)

    def body(b, carry):
        o = pl.multiple_of(b * W, W)
        before = pl.multiple_of(jnp.maximum(b - 1, 0) * W, W)
        after = pl.multiple_of(jnp.minimum(b + 1, N // W - 1) * W, W)
        second = lax.rem(b, 2) == 1
        rest = dot(last_ref[...], row_ref[...])
        u_ref[pl.ds(before, W), :] = jnp.where(lane >= o, rest, u_ref[pl.ds(before, W), :])
        above = jnp.where(second, u_ref[pl.ds(before, W), pl.ds(o, W)], 0.0)
        row_ref[...] = s_ref[pl.ds(o, W), :] - dot(above, u_ref[pl.ds(before, W), :], 0, 0)
        upper, inverse = factor(d_ref[...])
        u_ref[pl.ds(o, W), pl.ds(o, W)] = upper
        v_ref[pl.ds(o, W), pl.ds(pl.multiple_of((b % 2) * W, W), W)] = inverse
        last_ref[...] = inverse

        @pl.when(jnp.logical_not(second))
        def _():
            beside = dot(inverse, row_ref[:, pl.ds(after, W)])
            d_ref[...] = s_ref[pl.ds(after, W), pl.ds(after, W)] - dot(beside, beside, 0, 0)

        for k in range(PANELS - 1):

            @pl.when(b == 2 * k + 1)
            def _():
                e = NB * (k + 1)
                u_ref[e - W : e, e:] = dot(inverse, row_ref[:, e:])
                for f in range(e, N, NB):
                    above = u_ref[e - NB : e, f : f + NB]
                    s_ref[f : f + NB, f:] = s_ref[f : f + NB, f:] - dot(above, u_ref[e - NB : e, f:], 0, 0)
                d_ref[...] = s_ref[e : e + W, e : e + W]

        return carry

    lax.fori_loop(0, N // W, body, 0)
    for k in range(PANELS):
        o, m = NB * k, NB * k + W
        cross = dot(u_ref[o : o + W, m : m + W], v_ref[o : o + W, 0:W], 0, 0)
        v_ref[m : m + W, 0:W] = -dot(v_ref[m : m + W, W:NB], cross)


def update_kernel(place_ref, t_ref, upper_ref, inverse_ref, m_ref, o_ref, w_ref, u_ref, v_ref, sems):
    i, c = place_ref[0], place_ref[1]
    own = pl.ds(pl.multiple_of(jnp.minimum(i, PANELS - 1) * NB, NB), NB)
    factors = pltpu.make_async_copy(upper_ref.at[:, own], u_ref.at[:, 0:NB], sems.at[1, 0])
    arrivals = []
    for k in range(PANELS):
        o = NB * k
        arrivals.append([pltpu.make_async_copy(inverse_ref.at[o : o + NB], v_ref.at[o : o + NB], sems.at[0, k])])
        if k:
            arrivals[k].append(
                pltpu.make_async_copy(upper_ref.at[0:o, o : o + NB], u_ref.at[0:o, o : o + NB], sems.at[1, k])
            )
        for arrival in arrivals[k]:
            arrival.start()

    @pl.when(i < PANELS)
    def _():
        factors.start()

    for k in range(PANELS):
        o = NB * k
        for arrival in arrivals[k]:
            arrival.wait()
        t = jnp.concatenate([t_ref[:, k, n, :, :].reshape(NB, NB) for n in range(3)], 1)
        if k:
            t = t - dot(u_ref[0:o, o : o + NB], w_ref[0:o, :], 0, 0)
        w_ref[o : o + NB, :] = dot(v_ref[o : o + NB, :], t)

    @pl.when(i < PANELS)
    def _():
        factors.wait()
        w_ref[:, 2 * NB :] = u_ref[:, 0:NB]

    product = dot(w_ref[:, 2 * NB :], w_ref[:, : 2 * NB], 0, 0)
    keep = i >= PANELS
    o_ref[1] = jnp.where(keep, m_ref[1] - product[:, NB:], 0.0)

    @pl.when(c >= PANELS)
    def _():
        o_ref[0] = jnp.where(keep, m_ref[0] - product[:, :NB], 0.0)

    @pl.when(c < PANELS)
    def _():
        o_ref[0] = w_ref[pl.ds(pl.multiple_of(jnp.minimum(c, PANELS - 1) * NB, NB), NB), 2 * NB :].T


def copies(array, count):
    return jnp.broadcast_to(array[None], (count,) + array.shape)


def shards(matrix):
    rows_n = lax.axis_size("row")
    my_row = lax.axis_index("row")
    my_col = lax.axis_index("col")
    step = NB // rows_n
    mine = matrix[0].transpose(1, 0, 2)
    pieces = mine.reshape(2, rows_n, step, NB).transpose(1, 0, 2, 3)
    pieces = lax.all_to_all(pieces, "row", 0, 0)[:PANELS]
    wide = lax.all_gather(pieces, "col")
    head = jnp.concatenate([wide[c, : c + 1, 0] for c in range(PANELS)])
    halves = head.reshape(len(UPPER), step, 2, W).transpose(2, 0, 1, 3)
    lead = copies(halves, rows_n // 2).reshape(rows_n, len(UPPER), step, W)
    lead = lax.all_to_all(lead, "row", 0, 0)
    theirs = wide.transpose(2, 0, 1, 3, 4).reshape(rows_n, PANELS, 1, step, NB)
    tops = jnp.concatenate([copies(pieces, rows_n), theirs], 2)
    place = jnp.stack([my_row, my_col]).astype(jnp.int32)
    lead, tops, place = lax.optimization_barrier((lead, tops, place))
    tops = lax.all_to_all(tops, "row", 0, 0)
    other = lax.ppermute(lead, "row", [(i, i ^ 1) for i in range(rows_n)])
    f32 = jnp.float32
    hbm = pl.BlockSpec(memory_space=pltpu.HBM)
    upper, inverse = pl.pallas_call(
        lead_kernel,
        out_shape=[jax.ShapeDtypeStruct((N, N), f32), jax.ShapeDtypeStruct((N, NB), f32)],
        in_specs=[pl.BlockSpec(memory_space=pltpu.SMEM), hbm, hbm],
        scratch_shapes=[
            pltpu.VMEM((2,) + lead.shape, f32),
            pltpu.VMEM((N, N), f32),
            pltpu.VMEM((W, W), f32),
            pltpu.VMEM((W, N), f32),
            pltpu.VMEM((W, W), f32),
            pltpu.SemaphoreType.DMA((2,)),
        ],
        compiler_params=pltpu.CompilerParams(vmem_limit_bytes=55 << 20),
        cost_estimate=pl.CostEstimate(flops=2 << 30, bytes_accessed=100 << 20, transcendentals=0),
    )(place, lead, other)
    vmem = pl.BlockSpec(memory_space=pltpu.VMEM)
    out = pl.pallas_call(
        update_kernel,
        out_shape=jax.ShapeDtypeStruct((2, NB, NB), f32),
        in_specs=[pl.BlockSpec(memory_space=pltpu.SMEM), vmem, hbm, hbm, vmem],
        out_specs=vmem,
        scratch_shapes=[
            pltpu.VMEM((N, 3 * NB), f32),
            pltpu.VMEM((N, N), f32),
            pltpu.VMEM((N, NB), f32),
            pltpu.SemaphoreType.DMA((2, PANELS)),
        ],
        compiler_params=pltpu.CompilerParams(vmem_limit_bytes=24 << 20),
        cost_estimate=pl.CostEstimate(flops=2 << 30, bytes_accessed=8 << 20, transcendentals=0),
    )(place, tops, pltpu.with_memory_space_constraint(upper, pltpu.HBM), pltpu.with_memory_space_constraint(inverse, pltpu.HBM), mine)
    return out.transpose(1, 0, 2)[None]


def solution(mesh):
    spec = P(None, "row", None, "col")
    return jax.shard_map(shards, mesh=mesh, in_specs=(spec,), out_specs=spec, check_vma=False)
```

```python
import jax
import jax.numpy as jnp
from jax import lax
from jax.experimental import pallas as pl
from jax.experimental.pallas import tpu as pltpu
from jax.sharding import PartitionSpec as P

PANELS = 3
W = 128
NB = 256
N = PANELS * NB
UPPER = [(r, c) for c in range(PANELS) for r in range(c + 1)]


def dot(a, b, ca=1, cb=0):
    return lax.dot_general(
        a,
        b,
        (((ca,), (cb,)), ((), ())),
        precision=lax.Precision.HIGHEST,
        preferred_element_type=jnp.float32,
    )


def lane_of(x, k):
    return jnp.broadcast_to(x[:, k : k + 1], (8, W))


def row_of(x, s):
    return jnp.broadcast_to(x[s : s + 1, :], (8, W))


def factor(block):
    groups = W // 8
    half = groups // 2
    lane = lax.broadcasted_iota(jnp.int32, (8, W), 1)
    sub = lax.broadcasted_iota(jnp.int32, (8, W), 0)
    x = [block[8 * p : 8 * p + 8, :] for p in range(groups)]
    v = [jnp.where(lane == sub + 8 * p, 1.0, 0.0).astype(jnp.float32) for p in range(groups)]
    upper, inverse = [], []
    d = [lane_of(x[0], t) for t in range(8)]
    for p in range(groups):
        k = 8 * p
        later = range(p + 1, half if p < half else groups)
        c = {q: [lane_of(x[q], k + j) for j in range(8)] for q in later}
        ahead = [lane_of(x[p + 1], k + 8 + t) for t in range(8)] if later else None
        r = [row_of(x[p], j) for j in range(8)]
        z = [row_of(v[p], j) for j in range(8)]
        inv, root = [None] * 8, None
        for j in range(8):
            pivot = row_of(d[j], j)
            inv[j] = 1.0 / pivot
            root = lax.rsqrt(pivot) if j == 0 else jnp.where(sub == j, lax.rsqrt(pivot), root)
            for s in range(j + 1, 8):
                low = row_of(d[j], s) * inv[j]
                d[s] = d[s] - d[j] * low
                r[s] = r[s] - low * r[j]
                z[s] = z[s] - low * z[j]
                for q in later:
                    c[q][s] = c[q][s] - low * c[q][j]
        if later:
            for j in range(8):
                scaled = c[p + 1][j] * inv[j]
                for t in range(8):
                    ahead[t] = ahead[t] - c[p + 1][j] * row_of(scaled, t)
        sr = [r[j] * inv[j] for j in range(8)]
        sz = [z[j] * inv[j] for j in range(8)]
        for q in later:
            ax, av = c[q][0] * sr[0], c[q][0] * sz[0]
            for j in range(1, 8):
                ax, av = ax + c[q][j] * sr[j], av + c[q][j] * sz[j]
            x[q], v[q] = x[q] - ax, v[q] - av
        u, w = r[0], z[0]
        for j in range(1, 8):
            u, w = jnp.where(sub == j, r[j], u), jnp.where(sub == j, z[j], w)
        upper.append(jnp.where(lane >= sub + k, u * root, 0.0))
        inverse.append(w * root)
        d = ahead
        if p == half - 1:
            done = jnp.concatenate([jnp.concatenate(upper, 0), jnp.concatenate(inverse, 0)], 1)
            change = dot(done[:, 8 * half : W], done, 0, 0)
            for q in range(half, groups):
                rows = change[8 * (q - half) : 8 * (q - half) + 8]
                x[q], v[q] = x[q] - rows[:, :W], v[q] - rows[:, W:]
            d = [lane_of(x[half], 8 * half + t) for t in range(8)]
    return jnp.concatenate(upper, 0), jnp.concatenate(inverse, 0)


def lead_kernel(place_ref, mine_ref, other_ref, u_ref, v_ref, a_ref, s_ref, d_ref, row_ref, last_ref, sems):
    half = lax.rem(place_ref[0], 2)
    arrivals = [
        pltpu.make_async_copy(mine_ref, a_ref.at[half], sems.at[0]),
        pltpu.make_async_copy(other_ref, a_ref.at[1 - half], sems.at[1]),
    ]
    for arrival in arrivals:
        arrival.start()
    u_ref[...] = jnp.zeros_like(u_ref)
    v_ref[...] = jnp.zeros_like(v_ref)
    row_ref[...] = jnp.zeros_like(row_ref)
    last_ref[...] = jnp.zeros_like(last_ref)
    for arrival in arrivals:
        arrival.wait()
    for n, (r, c) in enumerate(UPPER):
        for h in range(2):
            o = NB * c + W * h
            s_ref[NB * r : NB * r + NB, o : o + W] = a_ref[h, :, n, :, :].reshape(NB, W)
    for r in range(1, PANELS):
        s_ref[NB * r : NB * r + NB, 0 : NB * r] = jnp.zeros((NB, NB * r), jnp.float32)
    d_ref[...] = s_ref[0:W, 0:W]
    lane = lax.broadcasted_iota(jnp.int32, (W, N), 1)

    def body(b, carry):
        o = pl.multiple_of(b * W, W)
        before = pl.multiple_of(jnp.maximum(b - 1, 0) * W, W)
        after = pl.multiple_of(jnp.minimum(b + 1, N // W - 1) * W, W)
        second = lax.rem(b, 2) == 1
        rest = dot(last_ref[...], row_ref[...])
        u_ref[pl.ds(before, W), :] = jnp.where(lane >= o, rest, u_ref[pl.ds(before, W), :])
        above = jnp.where(second, u_ref[pl.ds(before, W), pl.ds(o, W)], 0.0)
        row_ref[...] = s_ref[pl.ds(o, W), :] - dot(above, u_ref[pl.ds(before, W), :], 0, 0)
        upper, inverse = factor(d_ref[...])
        u_ref[pl.ds(o, W), pl.ds(o, W)] = upper
        v_ref[pl.ds(o, W), pl.ds(pl.multiple_of((b % 2) * W, W), W)] = inverse
        last_ref[...] = inverse

        @pl.when(jnp.logical_not(second))
        def _():
            beside = dot(inverse, row_ref[:, pl.ds(after, W)])
            d_ref[...] = s_ref[pl.ds(after, W), pl.ds(after, W)] - dot(beside, beside, 0, 0)

        for k in range(PANELS - 1):

            @pl.when(b == 2 * k + 1)
            def _():
                e = NB * (k + 1)
                u_ref[e - W : e, e:] = dot(inverse, row_ref[:, e:])
                for f in range(e, N, NB):
                    above = u_ref[e - NB : e, f : f + NB]
                    s_ref[f : f + NB, f:] = s_ref[f : f + NB, f:] - dot(above, u_ref[e - NB : e, f:], 0, 0)
                d_ref[...] = s_ref[e : e + W, e : e + W]

        return carry

    lax.fori_loop(0, N // W, body, 0)
    for k in range(PANELS):
        o, m = NB * k, NB * k + W
        cross = dot(u_ref[o : o + W, m : m + W], v_ref[o : o + W, 0:W], 0, 0)
        v_ref[m : m + W, 0:W] = -dot(v_ref[m : m + W, W:NB], cross)


def update_kernel(place_ref, t_ref, upper_ref, inverse_ref, mine_ref, o_ref, w_ref, u_ref, v_ref, m_ref, sems, late):
    i, c = place_ref[0], place_ref[1]
    own = pl.ds(pl.multiple_of(jnp.minimum(i, PANELS - 1) * NB, NB), NB)
    factors = pltpu.make_async_copy(upper_ref.at[:, own], u_ref.at[:, 0:NB], sems.at[1, 0])
    arrivals = []
    for k in range(PANELS):
        o = NB * k
        arrivals.append([pltpu.make_async_copy(inverse_ref.at[o : o + NB], v_ref.at[o : o + NB], sems.at[0, k])])
        if k:
            arrivals[k].append(
                pltpu.make_async_copy(upper_ref.at[0:o, o : o + NB], u_ref.at[0:o, o : o + NB], sems.at[1, k])
            )
        for arrival in arrivals[k]:
            arrival.start()

    matrix = pltpu.make_async_copy(mine_ref, m_ref, late)
    matrix.start()

    @pl.when(i < PANELS)
    def _():
        factors.start()

    for k in range(PANELS):
        o = NB * k
        for arrival in arrivals[k]:
            arrival.wait()
        t = jnp.concatenate([t_ref[:, k, n, :, :].reshape(NB, NB) for n in range(3)], 1)
        if k:
            t = t - dot(u_ref[0:o, o : o + NB], w_ref[0:o, :], 0, 0)
        w_ref[o : o + NB, :] = dot(v_ref[o : o + NB, :], t)

    @pl.when(i < PANELS)
    def _():
        factors.wait()
        w_ref[:, 2 * NB :] = u_ref[:, 0:NB]

    product = dot(w_ref[:, 2 * NB :], w_ref[:, : 2 * NB], 0, 0)
    matrix.wait()
    keep = i >= PANELS
    o_ref[1] = jnp.where(keep, m_ref[1] - product[:, NB:], 0.0)

    @pl.when(c >= PANELS)
    def _():
        o_ref[0] = jnp.where(keep, m_ref[0] - product[:, :NB], 0.0)

    @pl.when(c < PANELS)
    def _():
        o_ref[0] = w_ref[pl.ds(pl.multiple_of(jnp.minimum(c, PANELS - 1) * NB, NB), NB), 2 * NB :].T


def copies(array, count):
    return jnp.broadcast_to(array[None], (count,) + array.shape)


def shards(matrix):
    rows_n = lax.axis_size("row")
    my_row = lax.axis_index("row")
    my_col = lax.axis_index("col")
    step = NB // rows_n
    mine = matrix[0].transpose(1, 0, 2)
    pieces = mine.reshape(2, rows_n, step, NB).transpose(1, 0, 2, 3)
    pieces = lax.all_to_all(pieces, "row", 0, 0)[:PANELS]
    wide = lax.all_gather(pieces, "col")
    head = jnp.concatenate([wide[c, : c + 1, 0] for c in range(PANELS)])
    halves = head.reshape(len(UPPER), step, 2, W).transpose(2, 0, 1, 3)
    lead = copies(halves, rows_n // 2).reshape(rows_n, len(UPPER), step, W)
    lead = lax.all_to_all(lead, "row", 0, 0)
    theirs = wide.transpose(2, 0, 1, 3, 4).reshape(rows_n, PANELS, 1, step, NB)
    tops = jnp.concatenate([copies(pieces, rows_n), theirs], 2)
    place = jnp.stack([my_row, my_col]).astype(jnp.int32)
    lead, tops, place = lax.optimization_barrier((lead, tops, place))
    tops = lax.all_to_all(tops, "row", 0, 0)
    other = lax.ppermute(lead, "row", [(i, i ^ 1) for i in range(rows_n)])
    f32 = jnp.float32
    hbm = pl.BlockSpec(memory_space=pltpu.HBM)
    upper, inverse = pl.pallas_call(
        lead_kernel,
        out_shape=[jax.ShapeDtypeStruct((N, N), f32), jax.ShapeDtypeStruct((N, NB), f32)],
        in_specs=[pl.BlockSpec(memory_space=pltpu.SMEM), hbm, hbm],
        scratch_shapes=[
            pltpu.VMEM((2,) + lead.shape, f32),
            pltpu.VMEM((N, N), f32),
            pltpu.VMEM((W, W), f32),
            pltpu.VMEM((W, N), f32),
            pltpu.VMEM((W, W), f32),
            pltpu.SemaphoreType.DMA((2,)),
        ],
        compiler_params=pltpu.CompilerParams(vmem_limit_bytes=55 << 20),
        cost_estimate=pl.CostEstimate(flops=2 << 30, bytes_accessed=100 << 20, transcendentals=0),
    )(place, lead, other)
    vmem = pl.BlockSpec(memory_space=pltpu.VMEM)
    out = pl.pallas_call(
        update_kernel,
        out_shape=jax.ShapeDtypeStruct((2, NB, NB), f32),
        in_specs=[pl.BlockSpec(memory_space=pltpu.SMEM), vmem, hbm, hbm, hbm],
        out_specs=vmem,
        scratch_shapes=[
            pltpu.VMEM((N, 3 * NB), f32),
            pltpu.VMEM((N, N), f32),
            pltpu.VMEM((N, NB), f32),
            pltpu.VMEM((2, NB, NB), f32),
            pltpu.SemaphoreType.DMA((2, PANELS)),
            pltpu.SemaphoreType.DMA,
        ],
        compiler_params=pltpu.CompilerParams(vmem_limit_bytes=24 << 20),
        cost_estimate=pl.CostEstimate(flops=2 << 30, bytes_accessed=8 << 20, transcendentals=0),
    )(place, tops, pltpu.with_memory_space_constraint(upper, pltpu.HBM), pltpu.with_memory_space_constraint(inverse, pltpu.HBM), pltpu.with_memory_space_constraint(mine, pltpu.HBM))
    return out.transpose(1, 0, 2)[None]


def solution(mesh):
    spec = P(None, "row", None, "col")
    return jax.shard_map(shards, mesh=mesh, in_specs=(spec,), out_specs=spec, check_vma=False)
```
